128 devices in a mesh: pos: 2 (over y_hi), tv: 8 (over x, core), sv: 8 (over y_lo, z).
Axes of the slice: x: 4, y: 4 (y_hi: 2, y_lo: 2; y = y_hi * 2 + y_lo), z: 4, core: 2. Of those that a mesh axis runs over, the one named last changes fastest.
Arguments:
- teacher_hidden: bfloat16 [1024, 8192], P(None, 'pos')
- teacher_head: bfloat16 [8192, 81920], P('pos', ('tv', 'sv')), may hold values from -0.19824219 to 0.19824219
- align_pos: int32 [1024], replicated, may hold values from 0 to 1023, as said below
- pair_teacher: int32 [3072], P(('tv', 'sv')), may hold values from 0 to 9, as said below
- pair_student: int32 [3072], P(('tv', 'sv')), may hold values from 0 to 511, as said below
- align_values: bfloat16 [3072, 128, 128], P(('tv', 'sv'))
- student_hidden: bfloat16 [1024, 4096], P(None, 'pos')
- student_head: bfloat16 [4096, 65536], P('pos', ('tv', 'sv')), may hold values from -0.28125 to 0.28125
Outputs:
- row_loss: float32 [1024], P('pos')
- head_grad: bfloat16 [4096, 65536], P('pos', ('tv', 'sv'))
The draws below stay inside these ranges and needn't reach their ends.
Inputs may be any that keep to these rules, and one draw needn't show every extreme that they name: `align_pos`: nondecreasing. Entry k names teacher block (k // 48) * 10 + pair_teacher[k]. `pair_student`: the student blocks b of a pair list's entries (k // 48) * 48 to (k // 48) * 48 + 47 have at most 2 entries with the same b // 8; this bound is reached.
All inputs are finite; a program needn't handle non-finite values.
Results may differ from the reference program's by a relative error of at most 0.0048.
Values may be sent and summed in bfloat16 or wider, within the bound.
No kernel may reach another device: no remote copies, remote signals or barrier semaphores. Data moves between devices by JAX's collectives and lax.ppermute only.
A program may use at most 192 MiB of HBM per device.

```python
import jax
import jax.numpy as jnp
from jax import lax

DT = 8192
VT = 81920
DS = 4096
VS = 65536
BLOCK = 128
CAP = 2
POS = 1024
NBT = 640
NBS = 512
TB_DEV = 10
SB_DEV = 8
PAIR_DEV = 48
NPAIR = 3072


def draw_teacher_hidden(key, part):
    scale_key, value_key = jax.random.split(jax.random.fold_in(key, 11), 2)
    scales = 0.07 * jnp.exp(jax.random.uniform(scale_key, (POS, 1), jnp.float32, 0.0, jnp.log(10.0)))
    values = jax.random.normal(value_key, (POS, DT), jnp.float32)
    return (scales * values).astype(jnp.bfloat16)


def draw_student_hidden(key, part):
    scale_key, value_key = jax.random.split(jax.random.fold_in(key, 23), 2)
    scales = 0.07 * jnp.exp(jax.random.uniform(scale_key, (POS, 1), jnp.float32, 0.0, jnp.log(10.0)))
    values = jax.random.normal(value_key, (POS, DS), jnp.float32)
    return (scales * values).astype(jnp.bfloat16)


def draw_align_values(key, part):
    height = TB_DEV / PAIR_DEV
    columns = jnp.arange(BLOCK, dtype=jnp.int32)

    def one_tile(tile_key):
        keys = jax.random.split(tile_key, 7)
        main = jax.random.permutation(keys[0], BLOCK).astype(jnp.int32)
        first = jax.random.permutation(keys[1], BLOCK).astype(jnp.int32)
        second = jax.random.permutation(keys[2], BLOCK).astype(jnp.int32)
        keep_first = (jax.random.randint(keys[3], (BLOCK,), 0, 4, dtype=jnp.int32) > 0) & (first != main)
        keep_second = (jax.random.randint(keys[4], (BLOCK,), 0, 4, dtype=jnp.int32) > 0) & (second != main) & (second != first)
        main_value = jax.random.uniform(keys[5], (BLOCK,), jnp.float32, 0.6, 1.0)
        side_value = jax.random.uniform(keys[6], (BLOCK, 2), jnp.float32, 0.0, 0.28)
        tile = (main[:, None] == columns[None, :]).astype(jnp.float32) * main_value[:, None]
        tile = tile + ((first[:, None] == columns[None, :]) & keep_first[:, None]).astype(jnp.float32) * side_value[:, 0:1]
        tile = tile + ((second[:, None] == columns[None, :]) & keep_second[:, None]).astype(jnp.float32) * side_value[:, 1:2]
        return height * tile
    tiles = lax.map(one_tile, jax.random.split(jax.random.fold_in(key, 61), NPAIR))
    return tiles.astype(jnp.bfloat16)


def draw_align_pos(key, part):
    drawn = jnp.sort(jax.random.randint(jax.random.fold_in(key, 31), (POS,), 0, POS, dtype=jnp.int32))
    return drawn.at[0].set(0).at[POS - 1].set(POS - 1)


def draw_pair_teacher(key, part):
    owners = NPAIR // PAIR_DEV
    drawn = jax.random.randint(jax.random.fold_in(key, 41), (owners, PAIR_DEV), 0, TB_DEV, dtype=jnp.int32)
    drawn = drawn.at[:, 0].set(TB_DEV - 1).at[:, 1].set(0)
    return drawn.reshape(NPAIR)


def draw_pair_student(key, part):
    owners = NPAIR // PAIR_DEV
    slot_total = owners * CAP
    rank_key, noise_key, within_key, shuffle_key = jax.random.split(jax.random.fold_in(key, 53), 4)
    ranking = jax.random.permutation(rank_key, owners)
    heated = (ranking < owners // 4).astype(jnp.int32)
    slot_owner = jnp.arange(slot_total, dtype=jnp.int32) // CAP
    noise = jax.random.randint(noise_key, (owners, slot_total), 0, 65536, dtype=jnp.int32)
    scores = heated[slot_owner][None, :] * 67108864 + noise * 1024 + jnp.arange(slot_total, dtype=jnp.int32)[None, :]
    _, chosen = lax.top_k(scores, PAIR_DEV)
    row_keys = jax.random.split(shuffle_key, owners)
    chosen = jax.vmap(lambda row_key, row_slots: jax.random.permutation(row_key, row_slots))(row_keys, chosen)
    destination = chosen.astype(jnp.int32) // CAP
    within = jax.random.randint(within_key, (owners, PAIR_DEV), 0, SB_DEV, dtype=jnp.int32)
    return (destination * SB_DEV + within).reshape(NPAIR).astype(jnp.int32)


def level_of(rng, dims, pieces, smallest, largest):
    gain = 1.0
    for dim, parts in pieces:
        heights = jax.random.uniform(jax.random.fold_in(jax.random.fold_in(rng, 6), dim), (parts,), jnp.float32, smallest / len(pieces), largest / len(pieces))
        gain = gain * jnp.repeat(jnp.exp(heights), dims[dim] // parts).reshape((-1,) + (1,) * (len(dims) - 1 - dim))
    return gain


def gaussian(key, extent, spread, bound, shards=(), held_as=jnp.bfloat16):
    gain = level_of(key, extent, shards, -0.22, 0.18) if shards else 1.0
    values = jax.random.normal(key, extent, jnp.float32) * spread * gain
    return jnp.minimum(jnp.maximum(values, -bound), bound).astype(held_as)


def setup_inputs(seed: int = 0) -> dict:
    key_of = jax.random.split(jax.random.key(seed), 9)
    return {
        "teacher_hidden": draw_teacher_hidden(jax.random.fold_in(key_of[8], 71), 0),
        "teacher_head": gaussian(key_of[1], (DT, VT), (3.0 * DT ** -0.5), 0.19824219, ((0, 2), (1, 64))),
        "align_pos": draw_align_pos(jax.random.fold_in(key_of[8], 71), 0),
        "pair_teacher": draw_pair_teacher(jax.random.fold_in(key_of[8], 71), 0),
        "pair_student": draw_pair_student(jax.random.fold_in(key_of[8], 71), 0),
        "align_values": draw_align_values(jax.random.fold_in(key_of[8], 71), 0),
        "student_hidden": draw_student_hidden(jax.random.fold_in(key_of[8], 71), 0),
        "student_head": gaussian(key_of[7], (DS, VS), (3.0 * DS ** -0.5), 0.28125, ((0, 2), (1, 64))),
    }


loss_scale = 1024.0


def reference(teacher_hidden, teacher_head, align_pos, pair_teacher, pair_student, align_values, student_hidden, student_head):
    picked = jnp.take(teacher_hidden, align_pos, axis=0)
    teacher_logits = jnp.dot(picked, teacher_head, preferred_element_type=jnp.float32)
    teacher_max = jnp.max(teacher_logits, axis=1, keepdims=True)
    teacher_exp = jnp.exp(teacher_logits - teacher_max)
    teacher_prob = (teacher_exp / jnp.sum(teacher_exp, axis=1, keepdims=True)).astype(jnp.bfloat16)
    teacher_blocks = teacher_prob.reshape(POS, NBT, BLOCK)
    global_teacher = (jnp.arange(NPAIR, dtype=jnp.int32) // PAIR_DEV) * TB_DEV + pair_teacher

    def add_pair(pair_index, target):
        source = lax.dynamic_index_in_dim(teacher_blocks, global_teacher[pair_index], 1, keepdims=False)
        weights = lax.dynamic_index_in_dim(align_values, pair_index, 0, keepdims=False)
        product = jnp.dot(source, weights, preferred_element_type=jnp.float32)
        product = lax.optimization_barrier(product.astype(jnp.bfloat16)).astype(jnp.float32)
        current = lax.dynamic_index_in_dim(target, pair_student[pair_index], 1, keepdims=False)
        return lax.dynamic_update_index_in_dim(target, current + product, pair_student[pair_index], 1)

    target = lax.fori_loop(0, NPAIR, add_pair, jnp.zeros((POS, NBS, BLOCK), jnp.float32)).reshape(POS, VS)
    student_logits = jnp.dot(student_hidden, student_head, preferred_element_type=jnp.float32)
    student_peak = jnp.max(student_logits, axis=1)
    student_exp = jnp.exp(student_logits - student_peak[:, None])
    student_total = jnp.sum(student_exp, axis=1)
    mass = jnp.sum(target, axis=1)
    weighted = jnp.sum(target * student_logits, axis=1)
    row_loss = mass * (student_peak + jnp.log(student_total)) - weighted
    gradient = (loss_scale * (student_exp / student_total[:, None] * mass[:, None] - target)).astype(jnp.bfloat16)
    head_grad = jnp.dot(student_hidden.T, gradient, preferred_element_type=jnp.float32).astype(jnp.bfloat16)
    return (row_loss, head_grad)
```

```python
import jax
import jax.numpy as jnp
from jax import lax
from jax.experimental import pallas as pl
from jax.experimental.pallas import tpu as pltpu
from jax.sharding import PartitionSpec as P


loss_scale = 1024.0
LANES = 128
LEVELS = 32767.0
f32, bf16 = jnp.float32, jnp.bfloat16


def pieces(x):
    hi = x.astype(bf16).astype(f32)
    mid = (x - hi).astype(bf16).astype(f32)
    low = (x - hi - mid).astype(bf16).astype(f32)
    return hi, mid, low


def pieces_outside(x):
    hi = lax.reduce_precision(x, 8, 7)
    mid = lax.reduce_precision(x - hi, 8, 7)
    low = lax.reduce_precision(x - hi - mid, 8, 7)
    return hi, mid, low


def lane_of(shape):
    return lax.broadcasted_iota(jnp.int32, shape, len(shape) - 1)


def column_tile(columns, rows):
    lane = lane_of((rows, LANES))
    tile = jnp.zeros((rows, LANES), f32)
    for i, column in enumerate(columns):
        tile = jnp.where(lane == i, column, tile)
    return tile


def exp_kernel(own_ref, sent_ref, step_ref, codes_ref, out_ref):
    rows, width = own_ref.shape
    logits = own_ref[...] + sent_ref[...].astype(f32) * step_ref[...]
    peak = jnp.max(logits, axis=1, keepdims=True)
    powers = jnp.exp(logits - peak)
    total = jnp.sum(powers, axis=1, keepdims=True)
    out_ref[:, :width] = powers.astype(bf16)
    stats = column_tile(pieces(peak) + pieces(total), rows)
    out_ref[:, width:] = (stats + codes_ref[...].astype(f32)).astype(bf16)


def product_kernel(
    teacher_of, student_of, powers_ref, student_ref, *refs, owners, pairs, blocks, width
):
    values = refs[:owners]
    out_ref = refs[owners]
    held, total, weight, sems = refs[owners + 1 :]
    rows = powers_ref.shape[1]
    dests = out_ref.shape[0]
    copies = [
        pltpu.make_async_copy(values[j], held.at[j], sems.at[j]) for j in range(owners)
    ]
    for copy in copies:
        copy.start()

    chunk = blocks * rows

    @pl.loop(0, dests)
    def _(d):
        total[pl.ds(pl.multiple_of(d * chunk, chunk), chunk), :] = jnp.zeros((chunk, LANES), f32)

    peaks, sums = [], []
    for j in range(owners):
        tile = powers_ref[j, :, pl.ds(width, LANES)].astype(f32)
        peaks.append(tile[:, 0:1] + tile[:, 1:2] + tile[:, 2:3])
        sums.append(tile[:, 3:4] + tile[:, 4:5] + tile[:, 5:6])
    peak = peaks[0]
    for j in range(1, owners):
        peak = jnp.maximum(peak, peaks[j])
    norm = jnp.zeros_like(peak)
    for j in range(owners):
        factor = jnp.exp(peaks[j] - peak)
        norm = norm + sums[j] * factor
        weight[j] = jnp.broadcast_to(factor, (rows, LANES))

    group = 8
    for j in range(owners):
        copies[j].wait()

        @pl.loop(0, pairs // group)
        def _(i):
            products, places = [], []
            for u in range(group):
                k = i * group + u
                block = teacher_of[j * pairs + k]
                left = powers_ref[j, :, pl.ds(pl.multiple_of(block * LANES, LANES), LANES)]
                products.append(jnp.dot(left, held[j, k], preferred_element_type=f32))
                places.append(pl.multiple_of(student_of[j * pairs + k] * rows, rows))
            scale = weight[j]
            for product, place in zip(products, places):
                total[pl.ds(place, rows), :] += product * scale

    weight[0] = jnp.zeros((rows, LANES), f32)

    @pl.loop(0, dests)
    def _(d):
        part = weight[0]
        for b in range(blocks):
            here = total[pl.ds(pl.multiple_of((d * blocks + b) * rows, rows), rows), :]
            part = part + here
            out_ref[d, pl.ds(b * rows, rows), :] = here.astype(bf16)
        weight[0] = part

    mass = jnp.sum(weight[0], axis=1, keepdims=True)
    tile = column_tile(pieces(peak) + pieces(norm) + pieces(mass), rows)
    square = jnp.concatenate([tile, jnp.zeros((LANES - rows, LANES), f32)], axis=0)
    tail = jnp.concatenate(
        [jnp.transpose(square)[:16, :].astype(bf16), student_ref[...]], axis=0
    )

    @pl.loop(0, dests)
    def _(d):
        out_ref[d, pl.ds(chunk, tail.shape[0]), :] = tail


def gradient_kernel(
    main_ref, stats_ref, peak_ref, sum_ref, logits_ref, grad_ref, loss_ref, student, *, blocks
):
    step = pl.program_id(0)
    rows = grad_ref.shape[0]
    groups = main_ref.shape[0]

    @pl.when(step == 0)
    def _():
        part = peak_ref[...].astype(f32)
        peaks = part[:, 0:4] + part[:, 4:8] + part[:, 8:12]
        part = sum_ref[...].astype(f32)
        sums = part[:, 0:4] + part[:, 4:8] + part[:, 8:12]
        peak = jnp.max(peaks, axis=0)
        norm = jnp.sum(sums * jnp.exp(peaks - peak[None]), axis=0)
        for q in range(4):
            row = lax.broadcasted_iota(jnp.int32, (LANES, LANES), 0)
            tile = jnp.where(row == 0, peak[q : q + 1], jnp.where(row == 1, norm[q : q + 1], 0.0))
            student[q * LANES : (q + 1) * LANES, :] = jnp.transpose(tile)

    held = student[pl.ds(pl.multiple_of(step * rows, rows), rows), :]
    student_peak, student_total = held[:, 0:1], held[:, 1:2]
    stats = jnp.transpose(stats_ref[...].astype(f32).reshape(groups * 16, LANES))[:rows]

    def column(g, c):
        at = g * 16 + c
        return stats[:, at : at + 1] + stats[:, at + 1 : at + 2] + stats[:, at + 2 : at + 3]

    peaks = [column(g, 0) for g in range(groups)]
    peak = peaks[0]
    for other in peaks[1:]:
        peak = jnp.maximum(peak, other)
    powers = [jnp.exp(value - peak) for value in peaks]
    norm = sum(column(g, 3) * powers[g] for g in range(groups))
    factors = [power / norm for power in powers]
    mass = sum(column(g, 6) * factors[g] for g in range(groups))
    wide = [jnp.broadcast_to(factor, (rows, LANES)) for factor in factors]

    weighted = jnp.zeros((rows, LANES), f32)
    ratio = mass / student_total
    for b in range(blocks):
        target = jnp.zeros((rows, LANES), f32)
        for g in range(groups):
            target = target + main_ref[g, pl.ds(b * rows, rows), :].astype(f32) * wide[g]
        logits = logits_ref[:, b * LANES : (b + 1) * LANES]
        weighted = weighted + target * logits
        share = jnp.exp(logits - student_peak) * ratio
        grad_ref[:, b * LANES : (b + 1) * LANES] = (loss_scale * (share - target)).astype(bf16)
    base = mass * (student_peak + jnp.log(student_total))
    loss_ref[...] = column_tile((base, jnp.sum(weighted, axis=1, keepdims=True)), rows)


def coded(partial):
    step = jnp.max(jnp.abs(partial), axis=1, keepdims=True) / LEVELS
    inverse = jnp.where(step > 0, 1.0 / step, 0.0)
    return jnp.round(partial * inverse).astype(jnp.int32).astype(jnp.int16), step


def local(
    teacher_hidden,
    teacher_head,
    align_pos,
    pair_teacher,
    pair_student,
    align_values,
    student_hidden,
    student_head,
):
    pos = lax.axis_index("pos")
    group = lax.axis_size("tv")
    owners = group * lax.axis_size("sv")
    swap = [(0, 1), (1, 0)]
    count = align_pos.shape[0]
    half = count // 2
    pairs = pair_teacher.shape[0]
    width = teacher_head.shape[1]
    block = align_values.shape[1]
    blocks = student_head.shape[1] // block
    rows = half // group

    near = [align_values]
    for shift in (2, 6, 4):
        near.append(lax.ppermute(align_values, "tv", [(i, (i + shift) % group) for i in range(group)]))
    far = [lax.ppermute(v, "tv", [(i, i ^ 1) for i in range(group)]) for v in near]

    def picked(start):
        at = lax.dynamic_slice(align_pos, (start,), (half,))
        chosen = (at[:, None] == jnp.arange(count, dtype=jnp.int32)[None, :]).astype(bf16)
        return jnp.dot(chosen, teacher_hidden, preferred_element_type=f32).astype(bf16)

    def logits_of(start):
        return jnp.dot(picked(start), teacher_head, preferred_element_type=f32)

    own, other = pos * half, (1 - pos) * half
    sent, sent_step = coded(logits_of(other))
    got = lax.ppermute(sent, "pos", swap)
    got_step = lax.ppermute(sent_step, "pos", swap)
    own_logits = logits_of(own)

    codes = jnp.zeros((rows, LANES), bf16)
    listed = jnp.stack([pair_teacher, pair_student // 16, pair_student % 16]).astype(bf16)
    codes = lax.dynamic_update_slice(codes, listed, (0, 64))
    powers = pl.pallas_call(
        exp_kernel,
        grid=(group,),
        in_specs=[
            pl.BlockSpec((rows, width), lambda a: (a, 0)),
            pl.BlockSpec((rows, width), lambda a: (a, 0)),
            pl.BlockSpec((rows, 1), lambda a: (a, 0)),
            pl.BlockSpec((rows, LANES), lambda a: (0, 0)),
        ],
        out_specs=pl.BlockSpec((rows, width + LANES), lambda a: (a, 0)),
        out_shape=jax.ShapeDtypeStruct((half, width + LANES), bf16),
        name="teacher_exp",
    )(own_logits, got, got_step, codes)
    powers = lax.all_to_all(
        powers.reshape(group, rows, width + LANES), "tv", split_axis=0, concat_axis=0, tiled=True
    )

    def half_of(start):
        return lax.dynamic_slice(student_hidden, (start, 0), (half, student_hidden.shape[1]))

    student_sent, student_step = coded(
        jnp.dot(half_of(other), student_head, preferred_element_type=f32)
    )
    student_sent, student_step, _ = lax.optimization_barrier((student_sent, student_step, got))
    student_logits = jnp.dot(
        half_of(own), student_head, preferred_element_type=f32
    ) + lax.ppermute(student_sent, "pos", swap).astype(f32) * lax.ppermute(student_step, "pos", swap)
    peak = jnp.max(student_logits, axis=1)
    total = jnp.sum(jnp.exp(student_logits - peak[:, None]), axis=1)
    pad = jnp.zeros((4, LANES), f32)
    student_tail = jnp.concatenate(
        [p.reshape(4, LANES) for p in pieces_outside(peak)]
        + [pad]
        + [p.reshape(4, LANES) for p in pieces_outside(total)]
        + [pad]
    ).astype(bf16)

    place = lax.axis_index("tv")
    order = [place] + [(place - s) % group for s in (2, 6, 4)]
    order = jnp.stack(order + [o ^ 1 for o in order])
    powers = jnp.take(powers, order, axis=0, mode="clip")
    listed = powers[:, 0:3, width + 64 : width + 64 + pairs].astype(jnp.int32)
    teacher_of = listed[:, 0].reshape(-1)
    student_of = (listed[:, 1] * 16 + listed[:, 2]).reshape(-1)
    tall = blocks * rows + 48
    outgoing = pl.pallas_call(
        lambda *refs: product_kernel(*refs, owners=group, pairs=pairs, blocks=blocks, width=width),
        grid_spec=pltpu.PrefetchScalarGridSpec(
            num_scalar_prefetch=2,
            grid=(1,),
            in_specs=[
                pl.BlockSpec((group, rows, width + LANES), lambda i, *_: (0, 0, 0)),
                pl.BlockSpec((32, LANES), lambda i, *_: (0, 0)),
            ]
            + [pl.BlockSpec(memory_space=pl.ANY)] * group,
            out_specs=pl.BlockSpec(
                (owners, tall, LANES), lambda i, *_: (0, 0, 0), pipeline_mode=pl.Buffered(1)
            ),
            scratch_shapes=[
                pltpu.VMEM((group, pairs, block, block), bf16),
                pltpu.VMEM((owners * blocks * rows, LANES), f32),
                pltpu.VMEM((group, rows, LANES), f32),
                pltpu.SemaphoreType.DMA((group,)),
            ],
        ),
        out_shape=jax.ShapeDtypeStruct((owners, tall, LANES), bf16),
        compiler_params=pltpu.CompilerParams(vmem_limit_bytes=56 << 20),
        name="products",
    )(teacher_of, student_of, powers, student_tail, *near, *far)
    arrived = lax.all_to_all(outgoing, ("tv", "sv"), split_axis=0, concat_axis=0, tiled=True)

    per = owners // group
    gradient, loss = pl.pallas_call(
        lambda *refs: gradient_kernel(*refs, blocks=blocks),
        grid=(group,),
        in_specs=[
            pl.BlockSpec((per, blocks * rows, LANES), lambda a: (a, 0, 0)),
            pl.BlockSpec((per, 16, LANES), lambda a: (a, blocks * rows // 16, 0)),
            pl.BlockSpec((owners, 16, LANES), lambda a: (0, blocks * rows // 16 + 1, 0)),
            pl.BlockSpec((owners, 16, LANES), lambda a: (0, blocks * rows // 16 + 2, 0)),
            pl.BlockSpec((rows, blocks * block), lambda a: (a, 0)),
        ],
        out_specs=[
            pl.BlockSpec((rows, blocks * block), lambda a: (a, 0)),
            pl.BlockSpec((rows, LANES), lambda a: (a, 0)),
        ],
        out_shape=[
            jax.ShapeDtypeStruct((half, blocks * block), bf16),
            jax.ShapeDtypeStruct((half, LANES), f32),
        ],
        scratch_shapes=[pltpu.VMEM((half, LANES), f32)],
        name="logit_gradient",
    )(arrived, arrived, arrived, arrived, student_logits)

    other_gradient = lax.ppermute(gradient, "pos", swap)
    weighted = jnp.broadcast_to(loss[:, 1].reshape(1, 4, LANES), (owners, 4, LANES))
    weighted = lax.all_to_all(weighted, ("tv", "sv"), split_axis=0, concat_axis=0, tiled=True)
    row_loss = loss[:, 0] - jnp.sum(weighted, axis=0).reshape(half)

    def turned(start):
        return lax.optimization_barrier(jnp.transpose(half_of(start)))

    head_grad = jnp.dot(turned(own), gradient, preferred_element_type=f32) + jnp.dot(
        turned(other), other_gradient, preferred_element_type=f32
    )
    return (row_loss, head_grad.astype(bf16))


def solution(mesh):
    placed = (
        P(None, "pos"),
        P("pos", ("tv", "sv")),
        P(),
        P(("tv", "sv")),
        P(("tv", "sv")),
        P(("tv", "sv"), None, None),
        P(None, "pos"),
        P("pos", ("tv", "sv")),
    )
    return jax.shard_map(
        local,
        mesh=mesh,
        in_specs=placed,
        out_specs=(P("pos"), P("pos", ("tv", "sv"))),
        check_vma=False,
    )
```

```python
import jax
import jax.numpy as jnp
from jax import lax
from jax.experimental import pallas as pl
from jax.experimental.pallas import tpu as pltpu
from jax.sharding import PartitionSpec as P


loss_scale = 1024.0
LANES = 128
LEVELS = 32767.0
f32, bf16 = jnp.float32, jnp.bfloat16


def pieces(x):
    hi = x.astype(bf16).astype(f32)
    mid = (x - hi).astype(bf16).astype(f32)
    low = (x - hi - mid).astype(bf16).astype(f32)
    return hi, mid, low


def pieces_outside(x):
    hi = lax.reduce_precision(x, 8, 7)
    mid = lax.reduce_precision(x - hi, 8, 7)
    low = lax.reduce_precision(x - hi - mid, 8, 7)
    return hi, mid, low


def lane_of(shape):
    return lax.broadcasted_iota(jnp.int32, shape, len(shape) - 1)


def column_tile(columns, rows):
    lane = lane_of((rows, LANES))
    tile = jnp.zeros((rows, LANES), f32)
    for i, column in enumerate(columns):
        tile = jnp.where(lane == i, column, tile)
    return tile


def picked_logits_kernel(
    first, at_scalar, at_ref, hidden_ref, head_ref, *refs, tile, coded_out
):
    outs, (chosen, picked, total) = refs[:-3], refs[-3:]
    step = pl.program_id(0)
    count, depth = hidden_ref.shape
    rows = total.shape[0]
    part = 256

    @pl.when(step == 0)
    def _():
        @pl.loop(0, rows // tile)
        def _(i):
            line = at_ref[pl.ds(first[0] + i, 1), :].astype(f32)
            at = jnp.transpose(jnp.broadcast_to(line, (tile, LANES))).astype(jnp.int32)
            lane = lane_of((tile, LANES))
            for j in range(count // LANES):
                chosen[pl.ds(pl.multiple_of(i * tile, tile), tile), j * LANES : (j + 1) * LANES] = (
                    (at == lane + j * LANES).astype(f32).astype(bf16)
                )
        total[...] = jnp.zeros_like(total)

    @pl.loop(0, rows // tile)
    def _(i):
        here = pl.ds(pl.multiple_of(i * tile, tile), tile)
        low = at_scalar[(first[0] + i) * tile] // part
        high = at_scalar[(first[0] + i) * tile + tile - 1] // part

        def take(j):
            source = pl.ds(pl.multiple_of(j * part, part), part)
            return jnp.dot(chosen[here, source], hidden_ref[source, :], preferred_element_type=f32)

        picked[here, :] = take(low).astype(bf16)

        @pl.loop(low + 1, high + 1)
        def _(j):
            picked[here, :] = (picked[here, :].astype(f32) + take(j)).astype(bf16)

    total[...] += jnp.dot(picked[...], head_ref[...], preferred_element_type=f32)

    @pl.when(step == pl.num_programs(0) - 1)
    def _():
        if coded_out:
            partial = total[...]
            step_size = jnp.max(jnp.abs(partial), axis=1, keepdims=True) / LEVELS
            inverse = jnp.where(step_size > 0, 1.0 / step_size, 0.0)
            outs[0][...] = jnp.round(partial * inverse).astype(jnp.int32).astype(jnp.int16)
            outs[1][...] = jnp.broadcast_to(step_size, outs[1].shape)
        else:
            outs[0][...] = total[...]


def picked_logits(align_pos, hidden, head, start, half, coded_out):
    count, depth = hidden.shape
    width = head.shape[1]
    tile, chunk = LANES, 512
    shapes = [jax.ShapeDtypeStruct((half, width), jnp.int16 if coded_out else f32)]
    specs = [pl.BlockSpec((half, width), lambda k, *_: (0, 0))]
    if coded_out:
        shapes.append(jax.ShapeDtypeStruct((half, LANES), f32))
        specs.append(pl.BlockSpec((half, LANES), lambda k, *_: (0, 0)))
    return pl.pallas_call(
        lambda *refs: picked_logits_kernel(*refs, tile=tile, coded_out=coded_out),
        grid_spec=pltpu.PrefetchScalarGridSpec(
            num_scalar_prefetch=2,
            grid=(depth // chunk,),
            in_specs=[
                pl.BlockSpec((count // LANES, LANES), lambda k, *_: (0, 0)),
                pl.BlockSpec((count, chunk), lambda k, *_: (0, k)),
                pl.BlockSpec((chunk, width), lambda k, *_: (k, 0)),
            ],
            out_specs=specs,
            scratch_shapes=[
                pltpu.VMEM((half, count), bf16),
                pltpu.VMEM((half, chunk), bf16),
                pltpu.VMEM((half, width), f32),
            ],
        ),
        out_shape=shapes,
        cost_estimate=pl.CostEstimate(
            flops=2 * half * depth * width + half * count * depth,
            bytes_accessed=2 * depth * (count + width) + 4 * half * width,
            transcendentals=0,
        ),
        name="teacher_sent" if coded_out else "teacher_own",
    )((start // tile).reshape(1), align_pos, align_pos.reshape(-1, LANES), hidden, head)


def exp_kernel(own_ref, sent_ref, step_ref, codes_ref, out_ref):
    rows, width = own_ref.shape
    logits = own_ref[...] + sent_ref[...].astype(f32) * step_ref[:, 0:1]
    peak = jnp.max(logits, axis=1, keepdims=True)
    powers = jnp.exp(logits - peak)
    total = jnp.sum(powers, axis=1, keepdims=True)
    out_ref[:, :width] = powers.astype(bf16)
    stats = column_tile(pieces(peak) + pieces(total), rows)
    codes = jnp.concatenate([codes_ref[...].astype(f32)] * (rows // codes_ref.shape[0]), axis=0)
    out_ref[:, width:] = (stats + codes).astype(bf16)


def product_kernel(
    teacher_of, student_of, source_of, powers_ref, student_ref, *refs, owners, pairs, blocks, width
):
    values = refs[:owners]
    out_ref = refs[owners]
    held, total, weight, sems = refs[owners + 1 :]
    rows = powers_ref.shape[1]
    dests = out_ref.shape[0]
    for j in range(owners):
        pltpu.make_async_copy(values[j], held.at[j], sems.at[j]).start()

    chunk = blocks * rows

    @pl.loop(0, dests)
    def _(d):
        total[pl.ds(pl.multiple_of(d * chunk, chunk), chunk), :] = jnp.zeros((chunk, LANES), f32)

    couples = owners // 2
    peaks, sums = [], []
    for q in range(couples):
        tiles = [
            powers_ref[source_of[2 * q + i], :, pl.ds(width, LANES)].astype(f32) for i in range(2)
        ]
        turned = jnp.transpose(jnp.concatenate(tiles, axis=0))
        peaks.append(turned[0:1] + turned[1:2] + turned[2:3])
        sums.append(turned[3:4] + turned[4:5] + turned[5:6])
    peak = peaks[0]
    for other in peaks[1:]:
        peak = jnp.maximum(peak, other)
    peak = jnp.maximum(peak, pltpu.roll(peak, rows, 1))
    factors = [jnp.exp(value - peak) for value in peaks]
    norm = sum(factor * value for factor, value in zip(factors, sums))
    norm = norm + pltpu.roll(norm, rows, 1)
    line = lax.broadcasted_iota(jnp.int32, (LANES, LANES), 0)
    square = jnp.zeros((LANES, LANES), f32)
    for q in range(couples):
        square = jnp.where(line == q, factors[q], square)
    turned = jnp.transpose(square)
    for j in range(owners):
        top = (j % 2) * rows
        weight[j] = jnp.broadcast_to(turned[top : top + rows, j // 2 : j // 2 + 1], (rows, LANES))

    group = 8

    @pl.loop(0, owners)
    def _(j):
        pltpu.make_async_copy(values[0], held.at[j], sems.at[j]).wait()
        source = source_of[j]

        @pl.loop(0, pairs // group)
        def _(i):
            products, places = [], []
            for u in range(group):
                k = i * group + u
                block = teacher_of[source * pairs + k]
                left = powers_ref[source, :, pl.ds(pl.multiple_of(block * LANES, LANES), LANES)]
                products.append(jnp.dot(left, held[j, k], preferred_element_type=f32))
                places.append(pl.multiple_of(student_of[source * pairs + k] * rows, rows))
            scale = weight[j]
            for product, place in zip(products, places):
                total[pl.ds(place, rows), :] += product * scale

    weight[0] = jnp.zeros((rows, LANES), f32)

    @pl.loop(0, dests)
    def _(d):
        part = weight[0]
        for b in range(blocks):
            here = total[pl.ds(pl.multiple_of((d * blocks + b) * rows, rows), rows), :]
            part = part + here
            out_ref[d, pl.ds(b * rows, rows), :] = here.astype(bf16)
        weight[0] = part

    both = jnp.concatenate([weight[0], jnp.zeros((LANES - rows, LANES), f32)], axis=0)
    mass = jnp.sum(jnp.transpose(both), axis=0, keepdims=True)
    half_line = lax.broadcasted_iota(jnp.int32, (16, LANES), 0)
    stats = jnp.zeros((16, LANES), f32)
    for i, piece in enumerate(pieces(peak) + pieces(norm) + pieces(mass)):
        stats = jnp.where(half_line == i, piece, stats)
    tail = jnp.concatenate([stats.astype(bf16), student_ref[...]], axis=0)

    @pl.loop(0, dests)
    def _(d):
        out_ref[d, pl.ds(chunk, tail.shape[0]), :] = tail


def gradient_kernel(
    main_ref, stats_ref, peak_ref, sum_ref, logits_ref, grad_ref, loss_ref, student, *, blocks
):
    step = pl.program_id(0)
    rows = grad_ref.shape[0]
    groups = main_ref.shape[0]

    @pl.when(step == 0)
    def _():
        part = peak_ref[...].astype(f32)
        peaks = part[:, 0:4] + part[:, 4:8] + part[:, 8:12]
        part = sum_ref[...].astype(f32)
        sums = part[:, 0:4] + part[:, 4:8] + part[:, 8:12]
        peak = jnp.max(peaks, axis=0)
        norm = jnp.sum(sums * jnp.exp(peaks - peak[None]), axis=0)
        for q in range(4):
            row = lax.broadcasted_iota(jnp.int32, (LANES, LANES), 0)
            tile = jnp.where(row == 0, peak[q : q + 1], jnp.where(row == 1, norm[q : q + 1], 0.0))
            student[q * LANES : (q + 1) * LANES, :] = jnp.transpose(tile)

    part = stats_ref[...].astype(f32)

    def row(c):
        return part[:, c, :] + part[:, c + 1, :] + part[:, c + 2, :]

    peaks, norms, masses = row(0), row(3), row(6)
    powers = jnp.exp(peaks - jnp.max(peaks, axis=0, keepdims=True))
    factors = powers / jnp.sum(norms * powers, axis=0, keepdims=True)
    mass = jnp.sum(masses * factors, axis=0, keepdims=True)
    lines = jnp.concatenate(
        [factors, mass, jnp.zeros((LANES - groups - 1, LANES), f32)], axis=0
    )
    turned = jnp.transpose(lines)[:rows]
    held = student[pl.ds(pl.multiple_of(step * rows, rows), rows), :]
    student_peak, student_total = held[:, 0:1], held[:, 1:2]
    mass = turned[:, groups : groups + 1]
    wide = [jnp.broadcast_to(turned[:, g : g + 1], (rows, LANES)) for g in range(groups)]

    weighted = jnp.zeros((rows, LANES), f32)
    ratio = mass / student_total
    for b in range(blocks):
        target = jnp.zeros((rows, LANES), f32)
        for g in range(groups):
            target = target + main_ref[g, pl.ds(b * rows, rows), :].astype(f32) * wide[g]
        logits = logits_ref[:, b * LANES : (b + 1) * LANES]
        weighted = weighted + target * logits
        share = jnp.exp(logits - student_peak) * ratio
        grad_ref[:, b * LANES : (b + 1) * LANES] = (loss_scale * (share - target)).astype(bf16)
    base = mass * (student_peak + jnp.log(student_total))
    loss_ref[...] = column_tile((base, jnp.sum(weighted, axis=1, keepdims=True)), rows)


def coded(partial):
    step = jnp.max(jnp.abs(partial), axis=1, keepdims=True) / LEVELS
    inverse = jnp.where(step > 0, 1.0 / step, 0.0)
    return jnp.round(partial * inverse).astype(jnp.int32).astype(jnp.int16), step


def local(
    teacher_hidden,
    teacher_head,
    align_pos,
    pair_teacher,
    pair_student,
    align_values,
    student_hidden,
    student_head,
):
    pos = lax.axis_index("pos")
    group = lax.axis_size("tv")
    owners = group * lax.axis_size("sv")
    swap = [(0, 1), (1, 0)]
    count = align_pos.shape[0]
    half = count // 2
    pairs = pair_teacher.shape[0]
    width = teacher_head.shape[1]
    block = align_values.shape[1]
    blocks = student_head.shape[1] // block
    rows = half // group

    near = [align_values]
    for shift in (2, 6, 4):
        near.append(lax.ppermute(align_values, "tv", [(i, (i + shift) % group) for i in range(group)]))
    far = [lax.ppermute(v, "tv", [(i, i ^ 1) for i in range(group)]) for v in near]

    own, other = pos * half, (1 - pos) * half
    sent, sent_step = picked_logits(align_pos, teacher_hidden, teacher_head, other, half, True)
    got = lax.ppermute(sent, "pos", swap)
    got_step = lax.ppermute(sent_step, "pos", swap)
    (own_logits,) = picked_logits(align_pos, teacher_hidden, teacher_head, own, half, False)

    codes = jnp.zeros((rows, LANES), bf16)
    listed = jnp.stack([pair_teacher, pair_student // 16, pair_student % 16]).astype(bf16)
    codes = lax.dynamic_update_slice(codes, listed, (0, 64))
    powers = pl.pallas_call(
        exp_kernel,
        grid=(group // 2,),
        in_specs=[
            pl.BlockSpec((2 * rows, width), lambda a: (a, 0)),
            pl.BlockSpec((2 * rows, width), lambda a: (a, 0)),
            pl.BlockSpec((2 * rows, LANES), lambda a: (a, 0)),
            pl.BlockSpec((rows, LANES), lambda a: (0, 0)),
        ],
        out_specs=pl.BlockSpec((2 * rows, width + LANES), lambda a: (a, 0)),
        out_shape=jax.ShapeDtypeStruct((half, width + LANES), bf16),
        name="teacher_exp",
    )(own_logits, got, got_step, codes)
    powers = lax.all_to_all(
        powers.reshape(group, rows, width + LANES), "tv", split_axis=0, concat_axis=0, tiled=True
    )

    def half_of(start):
        return lax.dynamic_slice(student_hidden, (start, 0), (half, student_hidden.shape[1]))

    student_sent, student_step = coded(
        jnp.dot(half_of(other), student_head, preferred_element_type=f32)
    )
    student_sent, student_step, _ = lax.optimization_barrier((student_sent, student_step, got))
    student_logits = jnp.dot(
        half_of(own), student_head, preferred_element_type=f32
    ) + lax.ppermute(student_sent, "pos", swap).astype(f32) * lax.ppermute(student_step, "pos", swap)
    peak = jnp.max(student_logits, axis=1)
    total = jnp.sum(jnp.exp(student_logits - peak[:, None]), axis=1)
    pad = jnp.zeros((4, LANES), f32)
    student_tail = jnp.concatenate(
        [p.reshape(4, LANES) for p in pieces_outside(peak)]
        + [pad]
        + [p.reshape(4, LANES) for p in pieces_outside(total)]
        + [pad]
    ).astype(bf16)

    turned_own, turned_other, student_tail = lax.optimization_barrier(
        (jnp.transpose(half_of(own)), jnp.transpose(half_of(other)), student_tail)
    )

    place = lax.axis_index("tv")
    order = [place] + [(place - s) % group for s in (2, 6, 4)]
    order = jnp.stack(order + [o ^ 1 for o in order])
    listed = powers[:, 0:3, width + 64 : width + 64 + pairs].astype(jnp.int32)
    teacher_of = listed[:, 0].reshape(-1)
    student_of = (listed[:, 1] * 16 + listed[:, 2]).reshape(-1)
    tall = blocks * rows + 48
    outgoing = pl.pallas_call(
        lambda *refs: product_kernel(*refs, owners=group, pairs=pairs, blocks=blocks, width=width),
        grid_spec=pltpu.PrefetchScalarGridSpec(
            num_scalar_prefetch=3,
            grid=(1,),
            in_specs=[
                pl.BlockSpec((group, rows, width + LANES), lambda i, *_: (0, 0, 0)),
                pl.BlockSpec((32, LANES), lambda i, *_: (0, 0)),
            ]
            + [pl.BlockSpec(memory_space=pl.ANY)] * group,
            out_specs=pl.BlockSpec(
                (owners, tall, LANES), lambda i, *_: (0, 0, 0), pipeline_mode=pl.Buffered(1)
            ),
            scratch_shapes=[
                pltpu.VMEM((group, pairs, block, block), bf16),
                pltpu.VMEM((owners * blocks * rows, LANES), f32),
                pltpu.VMEM((group, rows, LANES), f32),
                pltpu.SemaphoreType.DMA((group,)),
            ],
        ),
        out_shape=jax.ShapeDtypeStruct((owners, tall, LANES), bf16),
        compiler_params=pltpu.CompilerParams(vmem_limit_bytes=56 << 20),
        name="products",
    )(teacher_of, student_of, order, powers, student_tail, *near, *far)
    arrived = lax.all_to_all(outgoing, ("tv", "sv"), split_axis=0, concat_axis=0, tiled=True)

    per = owners // group
    gradient, loss = pl.pallas_call(
        lambda *refs: gradient_kernel(*refs, blocks=blocks),
        grid=(group,),
        in_specs=[
            pl.BlockSpec((per, blocks * rows, LANES), lambda a: (a, 0, 0)),
            pl.BlockSpec((per, 16, LANES), lambda a: (a, blocks * rows // 16, 0)),
            pl.BlockSpec((owners, 16, LANES), lambda a: (0, blocks * rows // 16 + 1, 0)),
            pl.BlockSpec((owners, 16, LANES), lambda a: (0, blocks * rows // 16 + 2, 0)),
            pl.BlockSpec((rows, blocks * block), lambda a: (a, 0)),
        ],
        out_specs=[
            pl.BlockSpec((rows, blocks * block), lambda a: (a, 0)),
            pl.BlockSpec((rows, LANES), lambda a: (a, 0)),
        ],
        out_shape=[
            jax.ShapeDtypeStruct((half, blocks * block), bf16),
            jax.ShapeDtypeStruct((half, LANES), f32),
        ],
        scratch_shapes=[pltpu.VMEM((half, LANES), f32)],
        name="logit_gradient",
    )(arrived, arrived, arrived, arrived, student_logits)

    other_gradient = lax.ppermute(gradient, "pos", swap)
    own_part = jnp.dot(turned_own, gradient, preferred_element_type=f32)
    weighted = jnp.broadcast_to(loss[:, 1].reshape(1, 4, LANES), (owners, 4, LANES))
    weighted, own_part = lax.optimization_barrier((weighted, own_part))
    weighted = lax.all_to_all(weighted, ("tv", "sv"), split_axis=0, concat_axis=0, tiled=True)
    row_loss = loss[:, 0] - jnp.sum(weighted, axis=0).reshape(half)
    head_grad = own_part + jnp.dot(turned_other, other_gradient, preferred_element_type=f32)
    return (row_loss, head_grad.astype(bf16))


def solution(mesh):
    placed = (
        P(None, "pos"),
        P("pos", ("tv", "sv")),
        P(),
        P(("tv", "sv")),
        P(("tv", "sv")),
        P(("tv", "sv"), None, None),
        P(None, "pos"),
        P("pos", ("tv", "sv")),
    )
    return jax.shard_map(
        local,
        mesh=mesh,
        in_specs=placed,
        out_specs=(P("pos"), P("pos", ("tv", "sv"))),
        check_vma=False,
    )
```

```python
import jax
import jax.numpy as jnp
from jax import lax
from jax.experimental import pallas as pl
from jax.experimental.pallas import tpu as pltpu
from jax.sharding import PartitionSpec as P


loss_scale = 1024.0
LANES = 128
LEVELS = 32767.0
f32, bf16 = jnp.float32, jnp.bfloat16


def pieces(x):
    hi = x.astype(bf16).astype(f32)
    mid = (x - hi).astype(bf16).astype(f32)
    low = (x - hi - mid).astype(bf16).astype(f32)
    return hi, mid, low


def pieces_outside(x):
    hi = lax.reduce_precision(x, 8, 7)
    mid = lax.reduce_precision(x - hi, 8, 7)
    low = lax.reduce_precision(x - hi - mid, 8, 7)
    return hi, mid, low


def lane_of(shape):
    return lax.broadcasted_iota(jnp.int32, shape, len(shape) - 1)


def column_tile(columns, rows):
    lane = lane_of((rows, LANES))
    tile = jnp.zeros((rows, LANES), f32)
    for i, column in enumerate(columns):
        tile = jnp.where(lane == i, column, tile)
    return tile


def picked_logits_kernel(
    first, at_scalar, at_ref, hidden_ref, head_ref, *refs, tile, coded_out
):
    outs, (near, chosen, picked, total) = refs[:-4], refs[-4:]
    step = pl.program_id(0)
    count, depth = hidden_ref.shape
    rows, window = near.shape
    tiles = rows // tile
    part = 256

    lows = [at_scalar[(first[0] + i) * tile] for i in range(tiles)]
    highs = [at_scalar[(first[0] + i) * tile + tile - 1] for i in range(tiles)]
    bases = [jnp.minimum(lax.div(low, 16) * 16, count - window) for low in lows]
    narrow = highs[0] < bases[0] + window
    for base, high in zip(bases[1:], highs[1:]):
        narrow = jnp.logical_and(narrow, high < base + window)

    @pl.when(step == 0)
    def _():
        for i in range(tiles):
            line = at_ref[pl.ds(first[0] + i, 1), :].astype(f32)
            at = jnp.transpose(jnp.broadcast_to(line, (tile, LANES))).astype(jnp.int32)
            lane = lane_of((tile, LANES))
            here = slice(i * tile, (i + 1) * tile)
            for j in range(window // LANES):
                near[here, j * LANES : (j + 1) * LANES] = (
                    (at == lane + (j * LANES + bases[i])).astype(f32).astype(bf16)
                )

            @pl.when(jnp.logical_not(narrow))
            def _():
                for j in range(count // LANES):
                    chosen[here, j * LANES : (j + 1) * LANES] = (
                        (at == lane + j * LANES).astype(f32).astype(bf16)
                    )

        total[...] = jnp.zeros_like(total)

    @pl.when(narrow)
    def _():
        for i in range(tiles):
            here = slice(i * tile, (i + 1) * tile)
            source = pl.ds(pl.multiple_of(bases[i], 16), window)
            picked[here, :] = jnp.dot(
                near[here, :], hidden_ref[source, :], preferred_element_type=f32
            ).astype(bf16)
        total[...] += jnp.dot(picked[...], head_ref[...], preferred_element_type=f32)

    @pl.when(jnp.logical_not(narrow))
    def _():
        @pl.loop(0, tiles)
        def _(i):
            here = pl.ds(pl.multiple_of(i * tile, tile), tile)
            low = lax.div(at_scalar[(first[0] + i) * tile], part)
            high = lax.div(at_scalar[(first[0] + i) * tile + tile - 1], part)
            picked[here, :] = jnp.zeros((tile, depth), bf16)

            @pl.loop(low, high + 1)
            def _(j):
                source = pl.ds(pl.multiple_of(j * part, part), part)
                found = jnp.dot(
                    chosen[here, source], hidden_ref[source, :], preferred_element_type=f32
                )
                picked[here, :] = (picked[here, :].astype(f32) + found).astype(bf16)

        @pl.loop(0, head_ref.shape[1] // 256)
        def _(j):
            here = pl.ds(pl.multiple_of(j * 256, 256), 256)
            total[:, here] += jnp.dot(picked[...], head_ref[:, here], preferred_element_type=f32)

    @pl.when(step == pl.num_programs(0) - 1)
    def _():
        if not coded_out:
            outs[0][...] = total[...]
            return
        for i in range(tiles):
            here = slice(i * tile, (i + 1) * tile)
            partial = total[here, :]
            step_size = jnp.max(jnp.abs(partial), axis=1, keepdims=True) / LEVELS
            inverse = jnp.where(step_size > 0, 1.0 / step_size, 0.0)
            outs[0][here, :] = jnp.round(partial * inverse).astype(jnp.int32).astype(jnp.int16)
            turned = jnp.transpose(jnp.broadcast_to(step_size, (tile, LANES)))
            outs[1][i : i + 1, :] = turned[0:1]


def picked_logits(align_pos, hidden, head, start, half, coded_out):
    count, depth = hidden.shape
    width = head.shape[1]
    tile, chunk = LANES, 512
    shapes = [jax.ShapeDtypeStruct((half, width), jnp.int16 if coded_out else f32)]
    specs = [pl.BlockSpec((half, width), lambda k, *_: (0, 0))]
    if coded_out:
        shapes.append(jax.ShapeDtypeStruct((half // tile, LANES), f32))
        specs.append(pl.BlockSpec((half // tile, LANES), lambda k, *_: (0, 0)))
    return pl.pallas_call(
        lambda *refs: picked_logits_kernel(*refs, tile=tile, coded_out=coded_out),
        grid_spec=pltpu.PrefetchScalarGridSpec(
            num_scalar_prefetch=2,
            grid=(depth // chunk,),
            in_specs=[
                pl.BlockSpec((count // LANES, LANES), lambda k, *_: (0, 0)),
                pl.BlockSpec((count, chunk), lambda k, *_: (0, k)),
                pl.BlockSpec((chunk, width), lambda k, *_: (k, 0)),
            ],
            out_specs=specs,
            scratch_shapes=[
                pltpu.VMEM((half, min(256, count)), bf16),
                pltpu.VMEM((half, count), bf16),
                pltpu.VMEM((half, chunk), bf16),
                pltpu.VMEM((half, width), f32),
            ],
        ),
        out_shape=shapes,
        cost_estimate=pl.CostEstimate(
            flops=2 * half * depth * width + half * count * depth,
            bytes_accessed=2 * depth * (count + width) + 4 * half * width,
            transcendentals=0,
        ),
        name="teacher_sent" if coded_out else "teacher_own",
    )((start // tile).reshape(1), align_pos, align_pos.reshape(-1, LANES), hidden, head)


def exp_kernel(own_ref, sent_ref, step_ref, reach_ref, codes_ref, out_ref):
    rows, width = own_ref.shape
    line = step_ref[pl.ds(pl.program_id(0), 1), :]
    step_size = jnp.transpose(jnp.broadcast_to(line, (rows, LANES)))[:, 0:1]
    logits = own_ref[...] + sent_ref[...].astype(f32) * step_size
    peak = jnp.max(logits, axis=1, keepdims=True)
    powers = jnp.exp(logits - peak)
    total = jnp.sum(powers, axis=1, keepdims=True)
    out_ref[:, :width] = powers.astype(bf16)
    mass = jnp.sum(powers * reach_ref[...], axis=1, keepdims=True)
    stats = column_tile(pieces(peak) + pieces(total) + pieces(mass), rows)
    codes = jnp.concatenate([codes_ref[...].astype(f32)] * (rows // codes_ref.shape[0]), axis=0)
    out_ref[:, width:] = (stats + codes).astype(bf16)


FIELDS = 5


def product_kernel(codes, source_of, powers_ref, *refs, owners, pairs, blocks, width, upper):
    refs = list(refs)
    student_ref = None if upper else refs.pop(0)
    values, out_ref = refs[:owners], refs[owners]
    held, total, weight, sems = refs[owners + 1 :]
    rows = powers_ref.shape[1]
    dests = out_ref.shape[0]
    for j in range(owners):
        pltpu.make_async_copy(values[j], held.at[j], sems.at[j]).start()

    chunk = blocks * rows

    @pl.loop(0, dests)
    def _(d):
        total[pl.ds(pl.multiple_of(d * chunk, chunk), chunk), :] = jnp.zeros((chunk, LANES), f32)

    couples = owners // 2
    peaks, sums, masses = [], [], []
    for q in range(couples):
        tiles = [
            powers_ref[source_of[2 * q + i], :, pl.ds(width, LANES)].astype(f32) for i in range(2)
        ]
        turned = jnp.transpose(jnp.concatenate(tiles, axis=0))
        peaks.append(turned[0:1] + turned[1:2] + turned[2:3])
        sums.append(turned[3:4] + turned[4:5] + turned[5:6])
        masses.append(turned[6:7] + turned[7:8] + turned[8:9])
    peak = peaks[0]
    for other in peaks[1:]:
        peak = jnp.maximum(peak, other)
    peak = jnp.maximum(peak, pltpu.roll(peak, rows, 1))
    factors = [jnp.exp(value - peak) for value in peaks]
    line = lax.broadcasted_iota(jnp.int32, (LANES, LANES), 0)
    square = jnp.zeros((LANES, LANES), f32)
    for q in range(couples):
        square = jnp.where(line == q, factors[q], square)
    turned = jnp.transpose(square)
    for j in range(owners):
        top = (j % 2) * rows
        weight[j] = jnp.broadcast_to(turned[top : top + rows, j // 2 : j // 2 + 1], (rows, LANES))

    if not upper:
        both = [sum(f * v for f, v in zip(factors, values_)) for values_ in (sums, masses)]
        norm, mass = [value + pltpu.roll(value, rows, 1) for value in both]
        half_line = lax.broadcasted_iota(jnp.int32, (16, LANES), 0)
        stats = jnp.zeros((16, LANES), f32)
        for i, piece in enumerate(pieces(peak) + pieces(norm) + pieces(mass)):
            stats = jnp.where(half_line == i, piece, stats)
        tail = jnp.concatenate([stats.astype(bf16), student_ref[...]], axis=0)

        @pl.loop(0, dests)
        def _(d):
            out_ref[d, pl.ds(chunk, tail.shape[0]), :] = tail

    group = 8

    @pl.loop(0, owners)
    def _(j):
        pltpu.make_async_copy(values[0], held.at[j], sems.at[j]).wait()
        source = source_of[j]
        base = source * (FIELDS * pairs)
        lower = codes[base + 4 * pairs]
        first = lower if upper else 0
        last = pairs if upper else lower

        @pl.loop(0, lax.div(last - first + group - 1, group))
        def _(i):
            products, places = [], []
            scale = weight[j]
            for u in range(group):
                at = first + i * group + u
                k = base + jnp.minimum(at, pairs - 1)
                left = powers_ref[source, :, pl.ds(pl.multiple_of(codes[k] * LANES, LANES), LANES)]
                found = jnp.dot(left, held[j, codes[k + 3 * pairs]], preferred_element_type=f32)
                products.append(jnp.where(at < last, found * scale, 0.0))
                spot = codes[k + pairs] * blocks + codes[k + 2 * pairs]
                places.append(pl.multiple_of(spot * rows, rows))
            for product, place in zip(products, places):
                total[pl.ds(place, rows), :] += product

    @pl.loop(0, dests)
    def _(d):
        for b in range(blocks):
            here = total[pl.ds(pl.multiple_of((d * blocks + b) * rows, rows), rows), :]
            out_ref[d, pl.ds(b * rows, rows), :] = here.astype(bf16)


def product_call(codes, order, powers, tail, values, owners, blocks, width, upper):
    group, rows, wide = powers.shape
    pairs, block = values[0].shape[:2]
    tall = blocks * rows + (0 if upper else 48)
    return pl.pallas_call(
        lambda *refs: product_kernel(
            *refs, owners=group, pairs=pairs, blocks=blocks, width=width, upper=upper
        ),
        grid_spec=pltpu.PrefetchScalarGridSpec(
            num_scalar_prefetch=2,
            grid=(1,),
            in_specs=[pl.BlockSpec((group, rows, wide), lambda i, *_: (0, 0, 0))]
            + ([] if upper else [pl.BlockSpec((32, LANES), lambda i, *_: (0, 0))])
            + [pl.BlockSpec(memory_space=pl.ANY)] * group,
            out_specs=pl.BlockSpec(
                (owners, tall, LANES), lambda i, *_: (0, 0, 0), pipeline_mode=pl.Buffered(1)
            ),
            scratch_shapes=[
                pltpu.VMEM((group, pairs, block, block), bf16),
                pltpu.VMEM((owners * blocks * rows, LANES), f32),
                pltpu.VMEM((group, rows, LANES), f32),
                pltpu.SemaphoreType.DMA((group,)),
            ],
        ),
        out_shape=jax.ShapeDtypeStruct((owners, tall, LANES), bf16),
        compiler_params=pltpu.CompilerParams(vmem_limit_bytes=40 << 20),
        cost_estimate=pl.CostEstimate(
            flops=20 * group * pairs * rows * block * block,
            bytes_accessed=2 * group * pairs * block * block + 2 * owners * tall * LANES,
            transcendentals=0,
        ),
        name="products_upper" if upper else "products_lower",
    )(codes, order, powers, *([] if upper else [tail]), *values)


RATIO, PEAK, BASE, WEIGHTED = 8, 9, 10, 11


def gradient_kernel(*refs, blocks, upper):
    if upper:
        main_ref, kept_ref, logits_ref, grad_ref, loss_ref = refs
    else:
        main_ref, stats_ref, peak_ref, sum_ref, logits_ref, grad_ref, loss_ref, student = refs
    step = pl.program_id(0)
    rows = grad_ref.shape[0]
    groups = main_ref.shape[0]

    if upper:
        turned = kept_ref[...]
        student_peak, ratio = turned[:, PEAK : PEAK + 1], turned[:, RATIO : RATIO + 1]
        base, before = turned[:, BASE : BASE + 1], turned[:, WEIGHTED : WEIGHTED + 1]
    else:

        @pl.when(step == 0)
        def _():
            part = peak_ref[...].astype(f32)
            peaks = part[:, 0:4] + part[:, 4:8] + part[:, 8:12]
            part = sum_ref[...].astype(f32)
            sums = part[:, 0:4] + part[:, 4:8] + part[:, 8:12]
            peak = jnp.max(peaks, axis=0)
            norm = jnp.sum(sums * jnp.exp(peaks - peak[None]), axis=0)
            for q in range(4):
                row = lax.broadcasted_iota(jnp.int32, (LANES, LANES), 0)
                tile = jnp.where(row == 0, peak[q : q + 1], jnp.where(row == 1, norm[q : q + 1], 0.0))
                student[q * LANES : (q + 1) * LANES, :] = jnp.transpose(tile)

        part = stats_ref[...].astype(f32)

        def row(c):
            return part[:, c, :] + part[:, c + 1, :] + part[:, c + 2, :]

        peaks, norms, masses = row(0), row(3), row(6)
        powers = jnp.exp(peaks - jnp.max(peaks, axis=0, keepdims=True))
        factors = powers / jnp.sum(norms * powers, axis=0, keepdims=True)
        mass = jnp.sum(masses * factors, axis=0, keepdims=True)
        lines = jnp.concatenate(
            [factors, mass, jnp.zeros((LANES - groups - 1, LANES), f32)], axis=0
        )
        turned = jnp.transpose(lines)[:rows]
        held = student[pl.ds(pl.multiple_of(step * rows, rows), rows), :]
        student_peak, student_total = held[:, 0:1], held[:, 1:2]
        mass = turned[:, groups : groups + 1]
        ratio = mass / student_total
        base = mass * (student_peak + jnp.log(student_total))

    wide = [jnp.broadcast_to(turned[:, g : g + 1], (rows, LANES)) for g in range(groups)]
    weighted = jnp.zeros((rows, LANES), f32)
    for b in range(blocks):
        target = jnp.zeros((rows, LANES), f32)
        for g in range(groups):
            target = target + main_ref[g, pl.ds(b * rows, rows), :].astype(f32) * wide[g]
        logits = logits_ref[:, b * LANES : (b + 1) * LANES]
        weighted = weighted + target * logits
        share = jnp.exp(logits - student_peak) * ratio
        grad_ref[:, b * LANES : (b + 1) * LANES] = (loss_scale * (share - target)).astype(bf16)
    weighted = jnp.sum(weighted, axis=1, keepdims=True)
    if upper:
        loss_ref[...] = column_tile((base, weighted + before), rows)
    else:
        lane = lane_of((rows, LANES))
        kept = jnp.where(lane == RATIO, ratio, turned)
        kept = jnp.where(lane == PEAK, student_peak, kept)
        kept = jnp.where(lane == BASE, base, kept)
        loss_ref[...] = jnp.where(lane == WEIGHTED, weighted, kept)


def gradient_call(arrived, kept, logits, group, rows, blocks, upper):
    owners = arrived.shape[0]
    per = owners // group
    half, width = group * rows, blocks * LANES
    main = pl.BlockSpec((per, blocks * rows, LANES), lambda a: (a, 0, 0))
    at = blocks * rows // 16
    if upper:
        specs, args = [main, pl.BlockSpec((rows, LANES), lambda a: (a, 0))], [arrived, kept]
    else:
        specs = [
            main,
            pl.BlockSpec((per, 16, LANES), lambda a: (a, at, 0)),
            pl.BlockSpec((owners, 16, LANES), lambda a: (0, at + 1, 0)),
            pl.BlockSpec((owners, 16, LANES), lambda a: (0, at + 2, 0)),
        ]
        args = [arrived] * 4
    column = 1 if upper else 0
    return pl.pallas_call(
        lambda *refs: gradient_kernel(*refs, blocks=blocks, upper=upper),
        grid=(group,),
        in_specs=specs + [pl.BlockSpec((rows, width), lambda a: (a, column))],
        out_specs=[
            pl.BlockSpec((rows, width), lambda a: (a, 0)),
            pl.BlockSpec((rows, LANES), lambda a: (a, 0)),
        ],
        out_shape=[
            jax.ShapeDtypeStruct((half, width), bf16),
            jax.ShapeDtypeStruct((half, LANES), f32),
        ],
        scratch_shapes=[] if upper else [pltpu.VMEM((half, LANES), f32)],
        cost_estimate=pl.CostEstimate(
            flops=20 * owners * blocks * rows * LANES,
            bytes_accessed=3 * owners * blocks * rows * LANES,
            transcendentals=half * width,
        ),
        name="gradient_upper" if upper else "gradient_lower",
    )(*args, logits)


def head_kernel(own_hidden, other_hidden, own_ref, other_ref, *refs):
    out_ref = refs[-1]
    total = jnp.dot(own_hidden[...], own_ref[...], preferred_element_type=f32)
    total += jnp.dot(other_hidden[...], other_ref[...], preferred_element_type=f32)
    out_ref[...] = total.astype(bf16)


def head_call(own_hidden, other_hidden, own, other, before):
    depth, half = own_hidden.shape
    width = own.shape[1]
    tile = 512
    column = 0 if before is None else 1
    hidden = pl.BlockSpec((tile, half), lambda i: (i, 0))
    grad = pl.BlockSpec((half, width), lambda i: (0, 0))
    extra = [] if before is None else [before]
    return pl.pallas_call(
        head_kernel,
        grid=(depth // tile,),
        in_specs=[hidden, hidden, grad, grad] + [pl.BlockSpec(memory_space=pl.ANY)] * len(extra),
        out_specs=pl.BlockSpec((tile, width), lambda i: (i, column)),
        out_shape=jax.ShapeDtypeStruct((depth, 2 * width), bf16),
        input_output_aliases={4: 0} if extra else {},
        cost_estimate=pl.CostEstimate(
            flops=4 * depth * half * width, bytes_accessed=6 * depth * half, transcendentals=0
        ),
        name="head_upper" if extra else "head_lower",
    )(own_hidden, other_hidden, own, other, *extra)


def coded(partial):
    step = jnp.max(jnp.abs(partial), axis=1, keepdims=True) / LEVELS
    inverse = jnp.where(step > 0, 1.0 / step, 0.0)
    return jnp.round(partial * inverse).astype(jnp.int32).astype(jnp.int16), step


def local(
    teacher_hidden,
    teacher_head,
    align_pos,
    pair_teacher,
    pair_student,
    align_values,
    student_hidden,
    student_head,
):
    pos = lax.axis_index("pos")
    group = lax.axis_size("tv")
    owners = group * lax.axis_size("sv")
    swap = [(0, 1), (1, 0)]
    count = align_pos.shape[0]
    half = count // 2
    pairs = pair_teacher.shape[0]
    width = teacher_head.shape[1]
    block = align_values.shape[1]
    blocks = student_head.shape[1] // block
    rows = half // group

    near = [align_values]
    for shift in (2, 6, 4):
        near.append(lax.ppermute(align_values, "tv", [(i, (i + shift) % group) for i in range(group)]))
    far = [lax.ppermute(v, "tv", [(i, i ^ 1) for i in range(group)]) for v in near]

    own, other = pos * half, (1 - pos) * half
    sent, sent_step = picked_logits(align_pos, teacher_hidden, teacher_head, other, half, True)
    got = lax.ppermute(sent, "pos", swap)
    got_step = lax.ppermute(sent_step, "pos", swap)
    (own_logits,) = picked_logits(align_pos, teacher_hidden, teacher_head, own, half, False)

    lower_blocks = blocks // 2
    is_upper = (pair_student % blocks) // lower_blocks
    number = jnp.arange(pairs, dtype=jnp.int32)
    key = is_upper * pairs + number
    rank = jnp.sum((key[None, :] < key[:, None]).astype(jnp.int32), axis=1)
    fields = jnp.stack(
        [
            pair_teacher,
            pair_student // blocks,
            pair_student % lower_blocks,
            number,
            jnp.full_like(number, pairs) - jnp.sum(is_upper),
        ]
    )
    listed = jnp.sum(
        jnp.where(rank[None, None, :] == number[None, :, None], fields[:, None, :], 0), axis=2
    )
    listed = jnp.where(jnp.arange(FIELDS)[:, None] == FIELDS - 1, fields, listed).astype(bf16)
    codes = jnp.pad(listed, ((0, rows - FIELDS), (64, LANES - 64 - pairs)))
    row_sums = jnp.sum(align_values.astype(f32), axis=2)
    named = pair_teacher[None, :] == jnp.arange(width // block, dtype=jnp.int32)[:, None]
    reach = jnp.sum(jnp.where(named[:, :, None], row_sums[None], 0.0), axis=1).reshape(1, width)
    powers = pl.pallas_call(
        exp_kernel,
        grid=(group // 2,),
        in_specs=[
            pl.BlockSpec((2 * rows, width), lambda a: (a, 0)),
            pl.BlockSpec((2 * rows, width), lambda a: (a, 0)),
            pl.BlockSpec((group // 2, LANES), lambda a: (0, 0)),
            pl.BlockSpec((1, width), lambda a: (0, 0)),
            pl.BlockSpec((rows, LANES), lambda a: (0, 0)),
        ],
        out_specs=pl.BlockSpec((2 * rows, width + LANES), lambda a: (a, 0)),
        out_shape=jax.ShapeDtypeStruct((half, width + LANES), bf16),
        name="teacher_exp",
    )(own_logits, got, got_step, reach, codes)
    powers = lax.all_to_all(
        powers.reshape(group, rows, width + LANES), "tv", split_axis=0, concat_axis=0, tiled=True
    )

    def half_of(start):
        return lax.dynamic_slice(student_hidden, (start, 0), (half, student_hidden.shape[1]))

    student_sent, student_step = coded(
        jnp.dot(half_of(other), student_head, preferred_element_type=f32)
    )
    student_sent, student_step, _ = lax.optimization_barrier((student_sent, student_step, got))
    student_logits = jnp.dot(
        half_of(own), student_head, preferred_element_type=f32
    ) + lax.ppermute(student_sent, "pos", swap).astype(f32) * lax.ppermute(student_step, "pos", swap)
    peak = jnp.max(student_logits, axis=1)
    total = jnp.sum(jnp.exp(student_logits - peak[:, None]), axis=1)
    pad = jnp.zeros((4, LANES), f32)
    student_tail = jnp.concatenate(
        [p.reshape(4, LANES) for p in pieces_outside(peak)]
        + [pad]
        + [p.reshape(4, LANES) for p in pieces_outside(total)]
        + [pad]
    ).astype(bf16)

    turned_own, turned_other, student_tail = lax.optimization_barrier(
        (jnp.transpose(half_of(own)), jnp.transpose(half_of(other)), student_tail)
    )

    place = lax.axis_index("tv")
    order = [place] + [(place - s) % group for s in (2, 6, 4)]
    order = jnp.stack(order + [o ^ 1 for o in order])
    listed = powers[:, 0:FIELDS, width + 64 : width + 64 + pairs].astype(jnp.int32).reshape(-1)
    values = near + far

    def exchange(x):
        return lax.all_to_all(x, ("tv", "sv"), split_axis=0, concat_axis=0, tiled=True)

    lower = product_call(listed, order, powers, student_tail, values, owners, lower_blocks, width, False)
    lower = exchange(lower)
    upper = product_call(listed, order, powers, None, values, owners, lower_blocks, width, True)
    lower_grad, kept = gradient_call(lower, None, student_logits, group, rows, lower_blocks, False)
    upper = exchange(upper)
    lower_other = lax.ppermute(lower_grad, "pos", swap)
    head_grad = head_call(turned_own, turned_other, lower_grad, lower_other, None)
    upper, head_grad = lax.optimization_barrier((upper, head_grad))
    upper_grad, loss = gradient_call(upper, kept, student_logits, group, rows, lower_blocks, True)
    upper_other = lax.ppermute(upper_grad, "pos", swap)
    weighted = jnp.broadcast_to(loss[:, 1].reshape(1, 4, LANES), (owners, 4, LANES))
    row_loss = loss[:, 0] - jnp.sum(exchange(weighted), axis=0).reshape(half)
    head_grad = head_call(turned_own, turned_other, upper_grad, upper_other, head_grad)
    return (row_loss, head_grad)


def solution(mesh):
    placed = (
        P(None, "pos"),
        P("pos", ("tv", "sv")),
        P(),
        P(("tv", "sv")),
        P(("tv", "sv")),
        P(("tv", "sv"), None, None),
        P(None, "pos"),
        P("pos", ("tv", "sv")),
    )
    return jax.shard_map(
        local,
        mesh=mesh,
        in_specs=placed,
        out_specs=(P("pos"), P("pos", ("tv", "sv"))),
        check_vma=False,
    )
```

```python
import jax
import jax.numpy as jnp
from jax import lax
from jax.experimental import pallas as pl
from jax.experimental.pallas import tpu as pltpu
from jax.sharding import PartitionSpec as P


loss_scale = 1024.0
LANES = 128
LEVELS = 32767.0
f32, bf16 = jnp.float32, jnp.bfloat16


def pieces(x):
    hi = x.astype(bf16).astype(f32)
    mid = (x - hi).astype(bf16).astype(f32)
    low = (x - hi - mid).astype(bf16).astype(f32)
    return hi, mid, low


def pieces_outside(x):
    hi = lax.reduce_precision(x, 8, 7)
    mid = lax.reduce_precision(x - hi, 8, 7)
    low = lax.reduce_precision(x - hi - mid, 8, 7)
    return hi, mid, low


def lane_of(shape):
    return lax.broadcasted_iota(jnp.int32, shape, len(shape) - 1)


def column_tile(columns, rows):
    lane = lane_of((rows, LANES))
    tile = jnp.zeros((rows, LANES), f32)
    for i, column in enumerate(columns):
        tile = jnp.where(lane == i, column, tile)
    return tile


def picked_logits_kernel(
    first, at_scalar, at_ref, hidden_ref, head_ref, *refs, tile, coded_out
):
    outs, (near, chosen, picked, total) = refs[:-4], refs[-4:]
    step = pl.program_id(0)
    count, depth = hidden_ref.shape
    rows, window = near.shape
    tiles = rows // tile
    part = 256

    lows = [at_scalar[(first[0] + i) * tile] for i in range(tiles)]
    highs = [at_scalar[(first[0] + i) * tile + tile - 1] for i in range(tiles)]
    bases = [jnp.minimum(lax.div(low, 16) * 16, count - window) for low in lows]
    narrow = highs[0] < bases[0] + window
    for base, high in zip(bases[1:], highs[1:]):
        narrow = jnp.logical_and(narrow, high < base + window)

    @pl.when(step == 0)
    def _():
        for i in range(tiles):
            line = at_ref[pl.ds(first[0] + i, 1), :].astype(f32)
            at = jnp.transpose(jnp.broadcast_to(line, (tile, LANES))).astype(jnp.int32)
            lane = lane_of((tile, LANES))
            here = slice(i * tile, (i + 1) * tile)
            for j in range(window // LANES):
                near[here, j * LANES : (j + 1) * LANES] = (
                    (at == lane + (j * LANES + bases[i])).astype(f32).astype(bf16)
                )

            @pl.when(jnp.logical_not(narrow))
            def _():
                for j in range(count // LANES):
                    chosen[here, j * LANES : (j + 1) * LANES] = (
                        (at == lane + j * LANES).astype(f32).astype(bf16)
                    )

        total[...] = jnp.zeros_like(total)

    @pl.when(narrow)
    def _():
        for i in range(tiles):
            here = slice(i * tile, (i + 1) * tile)
            source = pl.ds(pl.multiple_of(bases[i], 16), window)
            picked[here, :] = jnp.dot(
                near[here, :], hidden_ref[source, :], preferred_element_type=f32
            ).astype(bf16)
        total[...] += jnp.dot(picked[...], head_ref[...], preferred_element_type=f32)

    @pl.when(jnp.logical_not(narrow))
    def _():
        @pl.loop(0, tiles)
        def _(i):
            here = pl.ds(pl.multiple_of(i * tile, tile), tile)
            low = lax.div(at_scalar[(first[0] + i) * tile], part)
            high = lax.div(at_scalar[(first[0] + i) * tile + tile - 1], part)
            picked[here, :] = jnp.zeros((tile, depth), bf16)

            @pl.loop(low, high + 1)
            def _(j):
                source = pl.ds(pl.multiple_of(j * part, part), part)
                found = jnp.dot(
                    chosen[here, source], hidden_ref[source, :], preferred_element_type=f32
                )
                picked[here, :] = (picked[here, :].astype(f32) + found).astype(bf16)

        @pl.loop(0, head_ref.shape[1] // 256)
        def _(j):
            here = pl.ds(pl.multiple_of(j * 256, 256), 256)
            total[:, here] += jnp.dot(picked[...], head_ref[:, here], preferred_element_type=f32)

    @pl.when(step == pl.num_programs(0) - 1)
    def _():
        if not coded_out:
            outs[0][...] = total[...]
            return
        for i in range(tiles):
            here = slice(i * tile, (i + 1) * tile)
            partial = total[here, :]
            step_size = jnp.max(jnp.abs(partial), axis=1, keepdims=True) / LEVELS
            inverse = jnp.where(step_size > 0, 1.0 / step_size, 0.0)
            outs[0][here, :] = jnp.round(partial * inverse).astype(jnp.int32).astype(jnp.int16)
            turned = jnp.transpose(jnp.broadcast_to(step_size, (tile, LANES)))
            outs[1][i : i + 1, :] = turned[0:1]


def picked_logits(align_pos, hidden, head, start, half, coded_out):
    count, depth = hidden.shape
    width = head.shape[1]
    tile, chunk = LANES, 512
    shapes = [jax.ShapeDtypeStruct((half, width), jnp.int16 if coded_out else f32)]
    specs = [pl.BlockSpec((half, width), lambda k, *_: (0, 0))]
    if coded_out:
        shapes.append(jax.ShapeDtypeStruct((half // tile, LANES), f32))
        specs.append(pl.BlockSpec((half // tile, LANES), lambda k, *_: (0, 0)))
    return pl.pallas_call(
        lambda *refs: picked_logits_kernel(*refs, tile=tile, coded_out=coded_out),
        grid_spec=pltpu.PrefetchScalarGridSpec(
            num_scalar_prefetch=2,
            grid=(depth // chunk,),
            in_specs=[
                pl.BlockSpec((count // LANES, LANES), lambda k, *_: (0, 0)),
                pl.BlockSpec((count, chunk), lambda k, *_: (0, k)),
                pl.BlockSpec((chunk, width), lambda k, *_: (k, 0)),
            ],
            out_specs=specs,
            scratch_shapes=[
                pltpu.VMEM((half, min(256, count)), bf16),
                pltpu.VMEM((half, count), bf16),
                pltpu.VMEM((half, chunk), bf16),
                pltpu.VMEM((half, width), f32),
            ],
        ),
        out_shape=shapes,
        cost_estimate=pl.CostEstimate(
            flops=2 * half * depth * width + half * count * depth,
            bytes_accessed=2 * depth * (count + width) + 4 * half * width,
            transcendentals=0,
        ),
        name="teacher_sent" if coded_out else "teacher_own",
    )((start // tile).reshape(1), align_pos, align_pos.reshape(-1, LANES), hidden, head)


def exp_kernel(own_ref, sent_ref, step_ref, reach_ref, codes_ref, out_ref):
    rows, width = own_ref.shape
    line = step_ref[pl.ds(pl.program_id(0), 1), :]
    step_size = jnp.transpose(jnp.broadcast_to(line, (rows, LANES)))[:, 0:1]
    logits = own_ref[...] + sent_ref[...].astype(f32) * step_size
    peak = jnp.max(logits, axis=1, keepdims=True)
    powers = jnp.exp(logits - peak)
    total = jnp.sum(powers, axis=1, keepdims=True)
    out_ref[:, :width] = powers.astype(bf16)
    mass = jnp.sum(powers * reach_ref[...], axis=1, keepdims=True)
    stats = column_tile(pieces(peak) + pieces(total) + pieces(mass), rows)
    codes = jnp.concatenate([codes_ref[...].astype(f32)] * (rows // codes_ref.shape[0]), axis=0)
    out_ref[:, width:] = (stats + codes).astype(bf16)


FIELDS = 3
STATS = 16


def product_kernel(codes, source_of, powers_ref, student_ref, *refs, owners, pairs, blocks, width):
    values, out_ref = refs[:owners], refs[owners]
    held, total, weight, staged, sems, out_sems = refs[owners + 1 :]
    rows = powers_ref.shape[1]
    dests = out_ref.shape[0]
    for j in range(owners):
        pltpu.make_async_copy(values[j], held.at[j], sems.at[j]).start()

    chunk = blocks * rows

    @pl.loop(0, dests)
    def _(d):
        total[pl.ds(pl.multiple_of(d * chunk, chunk), chunk), :] = jnp.zeros((chunk, LANES), f32)

    couples = owners // 2
    peaks, sums, masses = [], [], []
    for q in range(couples):
        tiles = [
            powers_ref[source_of[2 * q + i], :, pl.ds(width, LANES)].astype(f32) for i in range(2)
        ]
        turned = jnp.transpose(jnp.concatenate(tiles, axis=0))
        peaks.append(turned[0:1] + turned[1:2] + turned[2:3])
        sums.append(turned[3:4] + turned[4:5] + turned[5:6])
        masses.append(turned[6:7] + turned[7:8] + turned[8:9])
    peak = peaks[0]
    for other in peaks[1:]:
        peak = jnp.maximum(peak, other)
    peak = jnp.maximum(peak, pltpu.roll(peak, rows, 1))
    factors = [jnp.exp(value - peak) for value in peaks]
    norm = sum(f * v for f, v in zip(factors, sums))
    norm = norm + pltpu.roll(norm, rows, 1)
    factors = [factor / norm for factor in factors]
    mass = sum(f * v for f, v in zip(factors, masses))
    mass = mass + pltpu.roll(mass, rows, 1)
    level = peak + jnp.log(norm)
    line = lax.broadcasted_iota(jnp.int32, (LANES, LANES), 0)
    square = jnp.zeros((LANES, LANES), f32)
    for q in range(couples):
        square = jnp.where(line == q, factors[q], square)
    turned = jnp.transpose(square)
    for j in range(owners):
        top = (j % 2) * rows
        weight[j] = jnp.broadcast_to(turned[top : top + rows, j // 2 : j // 2 + 1], (rows, LANES))

    found = pieces(level) + pieces(mass)
    left_half = lane_of((1, LANES)) < rows
    half_line = lax.broadcasted_iota(jnp.int32, (STATS, LANES), 0)
    stats = student_ref[...].astype(f32)
    for i in range(3):
        both = jnp.where(left_half, found[2 * i], found[2 * i + 1])
        stats = jnp.where(half_line == 12 + i, both, stats)
    stats = stats.astype(bf16)

    group = 8

    @pl.loop(0, owners)
    def _(j):
        pltpu.make_async_copy(values[0], held.at[j], sems.at[j]).wait()
        source = source_of[j]
        base = source * (FIELDS * pairs)

        @pl.loop(0, pairs // group)
        def _(i):
            products, places = [], []
            for u in range(group):
                at = i * group + u
                k = base + at
                left = powers_ref[source, :, pl.ds(pl.multiple_of(codes[k] * LANES, LANES), LANES)]
                products.append(jnp.dot(left, held[j, at], preferred_element_type=f32))
                spot = codes[k + pairs] * blocks + codes[k + 2 * pairs]
                places.append(pl.multiple_of(spot * rows, rows))
            scale = weight[j]
            for product, place in zip(products, places):
                total[pl.ds(place, rows), :] += product * scale

    batch = staged.shape[1]
    slots = staged.shape[0]

    def send(n):
        return pltpu.make_async_copy(
            staged.at[n % slots], out_ref.at[pl.ds(n * batch, batch)], out_sems.at[n % slots]
        )

    for n in range(dests // batch):
        if n >= slots:
            send(n - slots).wait()
        slot = n % slots

        @pl.loop(0, batch)
        def _(d):
            for b in range(blocks):
                at = ((n * batch + d) * blocks + b) * rows
                here = total[pl.ds(pl.multiple_of(at, rows), rows), :]
                staged[slot, d, pl.ds(b * rows, rows), :] = here.astype(bf16)
            staged[slot, d, pl.ds(chunk, STATS), :] = stats

        send(n).start()
    for n in range(dests // batch - slots, dests // batch):
        send(n).wait()


def product_call(codes, order, powers, tail, values, owners, blocks, width):
    group, rows, wide = powers.shape
    pairs, block = values[0].shape[:2]
    tall = blocks * rows + STATS
    return pl.pallas_call(
        lambda *refs: product_kernel(*refs, owners=group, pairs=pairs, blocks=blocks, width=width),
        grid_spec=pltpu.PrefetchScalarGridSpec(
            num_scalar_prefetch=2,
            grid=(1,),
            in_specs=[
                pl.BlockSpec((group, rows, wide), lambda i, *_: (0, 0, 0)),
                pl.BlockSpec((STATS, LANES), lambda i, *_: (0, 0)),
            ]
            + [pl.BlockSpec(memory_space=pl.ANY)] * group,
            out_specs=pl.BlockSpec(memory_space=pl.ANY),
            scratch_shapes=[
                pltpu.VMEM((group, pairs, block, block), bf16),
                pltpu.VMEM((owners * blocks * rows, LANES), f32),
                pltpu.VMEM((group, rows, LANES), f32),
                pltpu.VMEM((2, 8, tall, LANES), bf16),
                pltpu.SemaphoreType.DMA((group,)),
                pltpu.SemaphoreType.DMA((2,)),
            ],
        ),
        out_shape=jax.ShapeDtypeStruct((owners, tall, LANES), bf16),
        compiler_params=pltpu.CompilerParams(vmem_limit_bytes=48 << 20),
        cost_estimate=pl.CostEstimate(
            flops=40 * group * pairs * rows * block * block,
            bytes_accessed=2 * group * pairs * block * block + 2 * owners * tall * LANES,
            transcendentals=0,
        ),
        name="products",
    )(codes, order, powers, tail, *values)


def gradient_kernel(
    main_ref, stats_ref, all_ref, logits_ref, low_ref, high_ref, loss_ref, student, *, blocks
):
    step = pl.program_id(0)
    rows = low_ref.shape[0]
    groups = main_ref.shape[0]

    @pl.when(step == 0)
    def _():
        part = all_ref[...].astype(f32)
        levels = part[:, 0:4] + part[:, 4:8] + part[:, 8:12]
        peak = jnp.max(levels, axis=0)
        level = peak + jnp.log(jnp.sum(jnp.exp(levels - peak[None]), axis=0))
        for q in range(4):
            tile = jnp.broadcast_to(level[q : q + 1], (LANES, LANES))
            student[q * LANES : (q + 1) * LANES, :] = jnp.transpose(tile)

    part = stats_ref[...].astype(f32)
    first, second, third = part[:, 12, :], part[:, 13, :], part[:, 14, :]
    levels = first + pltpu.roll(first, rows, 1) + second
    masses = pltpu.roll(second, rows, 1) + third + pltpu.roll(third, rows, 1)
    powers = jnp.exp(levels - jnp.max(levels, axis=0, keepdims=True))
    factors = powers / jnp.sum(powers, axis=0, keepdims=True)
    mass = jnp.sum(masses * factors, axis=0, keepdims=True)
    lines = jnp.concatenate([factors, mass, jnp.zeros((LANES - groups - 1, LANES), f32)], axis=0)
    turned = jnp.transpose(lines)[:rows]
    level = student[pl.ds(pl.multiple_of(step * rows, rows), rows), :]
    mass = turned[:, groups : groups + 1]
    wide = [jnp.broadcast_to(turned[:, g : g + 1], (rows, LANES)) for g in range(groups)]
    weighted = jnp.zeros((rows, LANES), f32)
    for b in range(blocks):
        target = jnp.zeros((rows, LANES), f32)
        for g in range(groups):
            target = target + main_ref[g, pl.ds(b * rows, rows), :].astype(f32) * wide[g]
        logits = logits_ref[:, b * LANES : (b + 1) * LANES]
        weighted = weighted + target * logits
        share = jnp.exp(logits - level) * mass
        grad_ref = low_ref if b < blocks // 2 else high_ref
        at = b % (blocks // 2) * LANES
        grad_ref[:, at : at + LANES] = (loss_scale * (share - target)).astype(bf16)
    weighted = jnp.sum(weighted, axis=1, keepdims=True)
    loss_ref[...] = column_tile((mass * level[:, 0:1], weighted), rows)


def gradient_call(arrived, logits, group, rows, blocks):
    owners = arrived.shape[0]
    per = owners // group
    half, width = group * rows, blocks // 2 * LANES
    at = blocks * rows // STATS
    return pl.pallas_call(
        lambda *refs: gradient_kernel(*refs, blocks=blocks),
        grid=(group,),
        in_specs=[
            pl.BlockSpec((per, blocks * rows, LANES), lambda a: (a, 0, 0)),
            pl.BlockSpec((per, STATS, LANES), lambda a: (a, at, 0)),
            pl.BlockSpec((owners, STATS, LANES), lambda a: (0, at, 0)),
            pl.BlockSpec((rows, 2 * width), lambda a: (a, 0)),
        ],
        out_specs=[
            pl.BlockSpec((rows, width), lambda a: (a, 0)),
            pl.BlockSpec((rows, width), lambda a: (a, 0)),
            pl.BlockSpec((rows, LANES), lambda a: (a, 0)),
        ],
        out_shape=[
            jax.ShapeDtypeStruct((half, width), bf16),
            jax.ShapeDtypeStruct((half, width), bf16),
            jax.ShapeDtypeStruct((half, LANES), f32),
        ],
        scratch_shapes=[pltpu.VMEM((half, LANES), f32)],
        cost_estimate=pl.CostEstimate(
            flops=20 * owners * blocks * rows * LANES,
            bytes_accessed=3 * owners * blocks * rows * LANES,
            transcendentals=2 * half * width,
        ),
        name="logit_gradient",
    )(arrived, arrived, arrived, logits)


def head_kernel(own_hidden, other_hidden, own_ref, other_ref, *refs):
    out_ref = refs[-1]
    total = jnp.dot(own_hidden[...], own_ref[...], preferred_element_type=f32)
    total += jnp.dot(other_hidden[...], other_ref[...], preferred_element_type=f32)
    out_ref[...] = total.astype(bf16)


def head_call(own_hidden, other_hidden, own, other, before):
    depth, half = own_hidden.shape
    width = own.shape[1]
    tile = 512
    column = 0 if before is None else 1
    hidden = pl.BlockSpec((tile, half), lambda i: (i, 0))
    grad = pl.BlockSpec((half, width), lambda i: (0, 0))
    extra = [] if before is None else [before]
    return pl.pallas_call(
        head_kernel,
        grid=(depth // tile,),
        in_specs=[hidden, hidden, grad, grad] + [pl.BlockSpec(memory_space=pl.ANY)] * len(extra),
        out_specs=pl.BlockSpec((tile, width), lambda i: (i, column)),
        out_shape=jax.ShapeDtypeStruct((depth, 2 * width), bf16),
        input_output_aliases={4: 0} if extra else {},
        cost_estimate=pl.CostEstimate(
            flops=4 * depth * half * width, bytes_accessed=6 * depth * half, transcendentals=0
        ),
        name="head_upper" if extra else "head_lower",
    )(own_hidden, other_hidden, own, other, *extra)


def coded(partial):
    step = jnp.max(jnp.abs(partial), axis=1, keepdims=True) / LEVELS
    inverse = jnp.where(step > 0, 1.0 / step, 0.0)
    return jnp.round(partial * inverse).astype(jnp.int32).astype(jnp.int16), step


def local(
    teacher_hidden,
    teacher_head,
    align_pos,
    pair_teacher,
    pair_student,
    align_values,
    student_hidden,
    student_head,
):
    pos = lax.axis_index("pos")
    group = lax.axis_size("tv")
    owners = group * lax.axis_size("sv")
    swap = [(0, 1), (1, 0)]
    count = align_pos.shape[0]
    half = count // 2
    pairs = pair_teacher.shape[0]
    width = teacher_head.shape[1]
    block = align_values.shape[1]
    blocks = student_head.shape[1] // block
    rows = half // group

    near = [align_values]
    for shift in (2, 6, 4):
        near.append(lax.ppermute(align_values, "tv", [(i, (i + shift) % group) for i in range(group)]))
    far = [lax.ppermute(v, "tv", [(i, i ^ 1) for i in range(group)]) for v in near]

    own, other = pos * half, (1 - pos) * half
    sent, sent_step = picked_logits(align_pos, teacher_hidden, teacher_head, other, half, True)
    got = lax.ppermute(sent, "pos", swap)
    got_step = lax.ppermute(sent_step, "pos", swap)
    (own_logits,) = picked_logits(align_pos, teacher_hidden, teacher_head, own, half, False)

    listed = jnp.stack([pair_teacher, pair_student // blocks, pair_student % blocks])
    listed = listed.astype(bf16)
    codes = jnp.pad(listed, ((0, rows - 3), (64, LANES - 64 - pairs)))
    row_sums = jnp.sum(align_values.astype(f32), axis=2)
    named = pair_teacher[None, :] == jnp.arange(width // block, dtype=jnp.int32)[:, None]
    reach = jnp.sum(jnp.where(named[:, :, None], row_sums[None], 0.0), axis=1).reshape(1, width)
    powers = pl.pallas_call(
        exp_kernel,
        grid=(group // 2,),
        in_specs=[
            pl.BlockSpec((2 * rows, width), lambda a: (a, 0)),
            pl.BlockSpec((2 * rows, width), lambda a: (a, 0)),
            pl.BlockSpec((group // 2, LANES), lambda a: (0, 0)),
            pl.BlockSpec((1, width), lambda a: (0, 0)),
            pl.BlockSpec((rows, LANES), lambda a: (0, 0)),
        ],
        out_specs=pl.BlockSpec((2 * rows, width + LANES), lambda a: (a, 0)),
        out_shape=jax.ShapeDtypeStruct((half, width + LANES), bf16),
        name="teacher_exp",
    )(own_logits, got, got_step, reach, codes)
    powers = lax.all_to_all(
        powers.reshape(group, rows, width + LANES), "tv", split_axis=0, concat_axis=0, tiled=True
    )

    def half_of(start):
        return lax.dynamic_slice(student_hidden, (start, 0), (half, student_hidden.shape[1]))

    student_sent, student_step = coded(
        jnp.dot(half_of(other), student_head, preferred_element_type=f32)
    )
    student_sent, student_step, _ = lax.optimization_barrier((student_sent, student_step, got))
    student_logits = jnp.dot(
        half_of(own), student_head, preferred_element_type=f32
    ) + lax.ppermute(student_sent, "pos", swap).astype(f32) * lax.ppermute(student_step, "pos", swap)
    peak = jnp.max(student_logits, axis=1)
    total = jnp.sum(jnp.exp(student_logits - peak[:, None]), axis=1)
    level = peak + jnp.log(total)
    student_tail = jnp.concatenate(
        [p.reshape(4, LANES) for p in pieces_outside(level)] + [jnp.zeros((4, LANES), f32)]
    ).astype(bf16)

    place = lax.axis_index("tv")
    order = [place] + [(place - s) % group for s in (2, 6, 4)]
    order = jnp.stack(order + [o ^ 1 for o in order])
    listed = powers[:, 0:FIELDS, width + 64 : width + 64 + pairs].astype(jnp.int32).reshape(-1)
    values = near + far

    def exchange(x):
        return lax.all_to_all(x, ("tv", "sv"), split_axis=0, concat_axis=0, tiled=True)

    outgoing = product_call(listed, order, powers, student_tail, values, owners, blocks, width)
    outgoing, hidden = lax.optimization_barrier((outgoing, student_hidden))
    arrived = exchange(outgoing)
    turned_own = jnp.transpose(lax.dynamic_slice(hidden, (own, 0), (half, hidden.shape[1])))
    turned_other = jnp.transpose(lax.dynamic_slice(hidden, (other, 0), (half, hidden.shape[1])))
    arrived, turned_own, turned_other = lax.optimization_barrier((arrived, turned_own, turned_other))
    lower_grad, upper_grad, loss = gradient_call(arrived, student_logits, group, rows, blocks)
    lower_other = lax.ppermute(lower_grad, "pos", swap)
    upper_other = lax.ppermute(upper_grad, "pos", swap)
    weighted = exchange(jnp.broadcast_to(loss[:, 1].reshape(1, 4, LANES), (owners, 4, LANES)))
    head_grad = head_call(turned_own, turned_other, lower_grad, lower_other, None)
    weighted, head_grad = lax.optimization_barrier((weighted, head_grad))
    row_loss = loss[:, 0] - jnp.sum(weighted, axis=0).reshape(half)
    head_grad = head_call(turned_own, turned_other, upper_grad, upper_other, head_grad)
    return (row_loss, head_grad)


def solution(mesh):
    placed = (
        P(None, "pos"),
        P("pos", ("tv", "sv")),
        P(),
        P(("tv", "sv")),
        P(("tv", "sv")),
        P(("tv", "sv"), None, None),
        P(None, "pos"),
        P("pos", ("tv", "sv")),
    )
    return jax.shard_map(
        local,
        mesh=mesh,
        in_specs=placed,
        out_specs=(P("pos"), P("pos", ("tv", "sv"))),
        check_vma=False,
    )
```

```python
import jax
import jax.numpy as jnp
from jax import lax
from jax.experimental import pallas as pl
from jax.experimental.pallas import tpu as pltpu
from jax.sharding import PartitionSpec as P


loss_scale = 1024.0
LANES = 128
LEVELS = 32767.0
f32, bf16 = jnp.float32, jnp.bfloat16


def pieces(x):
    hi = x.astype(bf16).astype(f32)
    mid = (x - hi).astype(bf16).astype(f32)
    low = (x - hi - mid).astype(bf16).astype(f32)
    return hi, mid, low


def pieces_outside(x):
    hi = lax.reduce_precision(x, 8, 7)
    mid = lax.reduce_precision(x - hi, 8, 7)
    low = lax.reduce_precision(x - hi - mid, 8, 7)
    return hi, mid, low


def lane_of(shape):
    return lax.broadcasted_iota(jnp.int32, shape, len(shape) - 1)


def column_tile(columns, rows):
    lane = lane_of((rows, LANES))
    tile = jnp.zeros((rows, LANES), f32)
    for i, column in enumerate(columns):
        tile = jnp.where(lane == i, column, tile)
    return tile


def picked_logits_kernel(
    first, at_scalar, at_ref, hidden_ref, head_ref, *refs, tile, coded_out
):
    outs, (near, chosen, picked, total) = refs[:-4], refs[-4:]
    step = pl.program_id(0)
    count, depth = hidden_ref.shape
    rows, window = near.shape
    tiles = rows // tile
    part = 256

    lows = [at_scalar[(first[0] + i) * tile] for i in range(tiles)]
    highs = [at_scalar[(first[0] + i) * tile + tile - 1] for i in range(tiles)]
    bases = [jnp.minimum(lax.div(low, 16) * 16, count - window) for low in lows]
    narrow = highs[0] < bases[0] + window
    for base, high in zip(bases[1:], highs[1:]):
        narrow = jnp.logical_and(narrow, high < base + window)

    @pl.when(step == 0)
    def _():
        for i in range(tiles):
            line = at_ref[pl.ds(first[0] + i, 1), :].astype(f32)
            at = jnp.transpose(jnp.broadcast_to(line, (tile, LANES))).astype(jnp.int32)
            lane = lane_of((tile, LANES))
            here = slice(i * tile, (i + 1) * tile)
            for j in range(window // LANES):
                near[here, j * LANES : (j + 1) * LANES] = (
                    (at == lane + (j * LANES + bases[i])).astype(f32).astype(bf16)
                )

            @pl.when(jnp.logical_not(narrow))
            def _():
                for j in range(count // LANES):
                    chosen[here, j * LANES : (j + 1) * LANES] = (
                        (at == lane + j * LANES).astype(f32).astype(bf16)
                    )

        total[...] = jnp.zeros_like(total)

    @pl.when(narrow)
    def _():
        for i in range(tiles):
            here = slice(i * tile, (i + 1) * tile)
            source = pl.ds(pl.multiple_of(bases[i], 16), window)
            picked[here, :] = jnp.dot(
                near[here, :], hidden_ref[source, :], preferred_element_type=f32
            ).astype(bf16)
        total[...] += jnp.dot(picked[...], head_ref[...], preferred_element_type=f32)

    @pl.when(jnp.logical_not(narrow))
    def _():
        @pl.loop(0, tiles)
        def _(i):
            here = pl.ds(pl.multiple_of(i * tile, tile), tile)
            low = lax.div(at_scalar[(first[0] + i) * tile], part)
            high = lax.div(at_scalar[(first[0] + i) * tile + tile - 1], part)
            picked[here, :] = jnp.zeros((tile, depth), bf16)

            @pl.loop(low, high + 1)
            def _(j):
                source = pl.ds(pl.multiple_of(j * part, part), part)
                found = jnp.dot(
                    chosen[here, source], hidden_ref[source, :], preferred_element_type=f32
                )
                picked[here, :] = (picked[here, :].astype(f32) + found).astype(bf16)

        @pl.loop(0, head_ref.shape[1] // 256)
        def _(j):
            here = pl.ds(pl.multiple_of(j * 256, 256), 256)
            total[:, here] += jnp.dot(picked[...], head_ref[:, here], preferred_element_type=f32)

    @pl.when(step == pl.num_programs(0) - 1)
    def _():
        if not coded_out:
            outs[0][...] = total[...]
            return
        for i in range(tiles):
            here = slice(i * tile, (i + 1) * tile)
            partial = total[here, :]
            step_size = jnp.max(jnp.abs(partial), axis=1, keepdims=True) / LEVELS
            inverse = jnp.where(step_size > 0, 1.0 / step_size, 0.0)
            outs[0][here, :] = jnp.round(partial * inverse).astype(jnp.int32).astype(jnp.int16)
            turned = jnp.transpose(jnp.broadcast_to(step_size, (tile, LANES)))
            outs[1][i : i + 1, :] = turned[0:1]


def picked_logits(align_pos, hidden, head, start, half, coded_out):
    count, depth = hidden.shape
    width = head.shape[1]
    tile, chunk = LANES, 1024
    shapes = [jax.ShapeDtypeStruct((half, width), jnp.int16 if coded_out else f32)]
    specs = [pl.BlockSpec((half, width), lambda k, *_: (0, 0))]
    if coded_out:
        shapes.append(jax.ShapeDtypeStruct((half // tile, LANES), f32))
        specs.append(pl.BlockSpec((half // tile, LANES), lambda k, *_: (0, 0)))
    return pl.pallas_call(
        lambda *refs: picked_logits_kernel(*refs, tile=tile, coded_out=coded_out),
        grid_spec=pltpu.PrefetchScalarGridSpec(
            num_scalar_prefetch=2,
            grid=(depth // chunk,),
            in_specs=[
                pl.BlockSpec((count // LANES, LANES), lambda k, *_: (0, 0)),
                pl.BlockSpec((count, chunk), lambda k, *_: (0, k)),
                pl.BlockSpec((chunk, width), lambda k, *_: (k, 0)),
            ],
            out_specs=specs,
            scratch_shapes=[
                pltpu.VMEM((half, min(256, count)), bf16),
                pltpu.VMEM((half, count), bf16),
                pltpu.VMEM((half, chunk), bf16),
                pltpu.VMEM((half, width), f32),
            ],
        ),
        out_shape=shapes,
        cost_estimate=pl.CostEstimate(
            flops=2 * half * depth * width + half * count * depth,
            bytes_accessed=2 * depth * (count + width) + 4 * half * width,
            transcendentals=0,
        ),
        name="teacher_sent" if coded_out else "teacher_own",
    )((start // tile).reshape(1), align_pos, align_pos.reshape(-1, LANES), hidden, head)


def exp_kernel(own_ref, sent_ref, step_ref, reach_ref, codes_ref, out_ref):
    rows, width = own_ref.shape
    line = step_ref[pl.ds(pl.program_id(0), 1), :]
    step_size = jnp.transpose(jnp.broadcast_to(line, (rows, LANES)))[:, 0:1]
    logits = own_ref[...] + sent_ref[...].astype(f32) * step_size
    peak = jnp.max(logits, axis=1, keepdims=True)
    powers = jnp.exp(logits - peak)
    total = jnp.sum(powers, axis=1, keepdims=True)
    out_ref[:, :width] = powers.astype(bf16)
    mass = jnp.sum(powers * reach_ref[...], axis=1, keepdims=True)
    stats = column_tile(pieces(peak) + pieces(total) + pieces(mass), rows)
    codes = jnp.concatenate([codes_ref[...].astype(f32)] * (rows // codes_ref.shape[0]), axis=0)
    out_ref[:, width:] = (stats + codes).astype(bf16)


FIELDS = 3
STATS = 16


def product_kernel(codes, source_of, powers_ref, student_ref, *refs, owners, pairs, blocks, width):
    values, out_ref = refs[:owners], refs[owners]
    held, total, weight, staged, sems, out_sems = refs[owners + 1 :]
    rows = powers_ref.shape[1]
    dests = out_ref.shape[0]
    for j in range(owners):
        pltpu.make_async_copy(values[j], held.at[j], sems.at[j]).start()

    chunk = blocks * rows

    @pl.loop(0, dests)
    def _(d):
        total[pl.ds(pl.multiple_of(d * chunk, chunk), chunk), :] = jnp.zeros((chunk, LANES), f32)

    couples = owners // 2
    peaks, sums, masses = [], [], []
    for q in range(couples):
        tiles = [
            powers_ref[source_of[2 * q + i], :, pl.ds(width, LANES)].astype(f32) for i in range(2)
        ]
        turned = jnp.transpose(jnp.concatenate(tiles, axis=0))
        peaks.append(turned[0:1] + turned[1:2] + turned[2:3])
        sums.append(turned[3:4] + turned[4:5] + turned[5:6])
        masses.append(turned[6:7] + turned[7:8] + turned[8:9])
    peak = peaks[0]
    for other in peaks[1:]:
        peak = jnp.maximum(peak, other)
    peak = jnp.maximum(peak, pltpu.roll(peak, rows, 1))
    factors = [jnp.exp(value - peak) for value in peaks]
    norm = sum(f * v for f, v in zip(factors, sums))
    norm = norm + pltpu.roll(norm, rows, 1)
    factors = [factor / norm for factor in factors]
    mass = sum(f * v for f, v in zip(factors, masses))
    mass = mass + pltpu.roll(mass, rows, 1)
    level = peak + jnp.log(norm)
    line = lax.broadcasted_iota(jnp.int32, (LANES, LANES), 0)
    square = jnp.zeros((LANES, LANES), f32)
    for q in range(couples):
        square = jnp.where(line == q, factors[q], square)
    turned = jnp.transpose(square)
    for j in range(owners):
        top = (j % 2) * rows
        weight[j] = jnp.broadcast_to(turned[top : top + rows, j // 2 : j // 2 + 1], (rows, LANES))

    found = pieces(level) + pieces(mass)
    left_half = lane_of((1, LANES)) < rows
    half_line = lax.broadcasted_iota(jnp.int32, (STATS, LANES), 0)
    stats = student_ref[...].astype(f32)
    for i in range(3):
        both = jnp.where(left_half, found[2 * i], found[2 * i + 1])
        stats = jnp.where(half_line == 12 + i, both, stats)
    stats = stats.astype(bf16)

    group = 8

    @pl.loop(0, owners)
    def _(j):
        pltpu.make_async_copy(values[0], held.at[j], sems.at[j]).wait()
        source = source_of[j]
        base = source * (FIELDS * pairs)

        @pl.loop(0, pairs // group)
        def _(i):
            products, places = [], []
            for u in range(group):
                at = i * group + u
                k = base + at
                left = powers_ref[source, :, pl.ds(pl.multiple_of(codes[k] * LANES, LANES), LANES)]
                products.append(jnp.dot(left, held[j, at], preferred_element_type=f32))
                spot = codes[k + pairs] * blocks + codes[k + 2 * pairs]
                places.append(pl.multiple_of(spot * rows, rows))
            scale = weight[j]
            for product, place in zip(products, places):
                total[pl.ds(place, rows), :] += product * scale

    batch = staged.shape[1]
    slots = staged.shape[0]

    def send(n):
        return pltpu.make_async_copy(
            staged.at[n % slots], out_ref.at[pl.ds(n * batch, batch)], out_sems.at[n % slots]
        )

    for n in range(dests // batch):
        if n >= slots:
            send(n - slots).wait()
        slot = n % slots

        @pl.loop(0, batch)
        def _(d):
            for b in range(blocks):
                at = ((n * batch + d) * blocks + b) * rows
                here = total[pl.ds(pl.multiple_of(at, rows), rows), :]
                staged[slot, d, pl.ds(b * rows, rows), :] = here.astype(bf16)
            staged[slot, d, pl.ds(chunk, STATS), :] = stats

        send(n).start()
    for n in range(dests // batch - slots, dests // batch):
        send(n).wait()


def product_call(codes, order, powers, tail, values, owners, blocks, width):
    group, rows, wide = powers.shape
    pairs, block = values[0].shape[:2]
    tall = blocks * rows + STATS
    return pl.pallas_call(
        lambda *refs: product_kernel(*refs, owners=group, pairs=pairs, blocks=blocks, width=width),
        grid_spec=pltpu.PrefetchScalarGridSpec(
            num_scalar_prefetch=2,
            grid=(1,),
            in_specs=[
                pl.BlockSpec((group, rows, wide), lambda i, *_: (0, 0, 0)),
                pl.BlockSpec((STATS, LANES), lambda i, *_: (0, 0)),
            ]
            + [pl.BlockSpec(memory_space=pl.ANY)] * group,
            out_specs=pl.BlockSpec(memory_space=pl.ANY),
            scratch_shapes=[
                pltpu.VMEM((group, pairs, block, block), bf16),
                pltpu.VMEM((owners * blocks * rows, LANES), f32),
                pltpu.VMEM((group, rows, LANES), f32),
                pltpu.VMEM((2, 8, tall, LANES), bf16),
                pltpu.SemaphoreType.DMA((group,)),
                pltpu.SemaphoreType.DMA((2,)),
            ],
        ),
        out_shape=jax.ShapeDtypeStruct((owners, tall, LANES), bf16),
        compiler_params=pltpu.CompilerParams(vmem_limit_bytes=48 << 20),
        cost_estimate=pl.CostEstimate(
            flops=40 * group * pairs * rows * block * block,
            bytes_accessed=2 * group * pairs * block * block + 2 * owners * tall * LANES,
            transcendentals=0,
        ),
        name="products",
    )(codes, order, powers, tail, *values)


def gradient_kernel(
    main_ref, all_ref, logits_ref, low_ref, high_ref, base_ref, loss_ref, columns, lines, *, blocks
):
    step = pl.program_id(0)
    rows = low_ref.shape[0]
    groups = main_ref.shape[0]
    chunks = all_ref.shape[0] // groups

    @pl.when(step == 0)
    def _():
        part = all_ref[...].astype(f32)
        levels = part[:, 0:4] + part[:, 4:8] + part[:, 8:12]
        peak = jnp.max(levels, axis=0)
        student = peak + jnp.log(jnp.sum(jnp.exp(levels - peak[None]), axis=0))
        other = pltpu.roll(student, rows, 1)
        first, second, third = part[:, 12, :], part[:, 13, :], part[:, 14, :]
        levels = first + pltpu.roll(first, rows, 1) + second
        masses = pltpu.roll(second, rows, 1) + third + pltpu.roll(third, rows, 1)
        for a in range(chunks):
            of = slice(a * groups, (a + 1) * groups)
            powers = jnp.exp(levels[of] - jnp.max(levels[of], axis=0, keepdims=True))
            factors = powers / jnp.sum(powers, axis=0, keepdims=True)
            mass = jnp.sum(masses[of] * factors, axis=0, keepdims=True)
            level = (other if a % 2 else student)[a // 2 : a // 2 + 1]
            base_ref[a : a + 1, :] = mass * level
            tile = jnp.concatenate(
                [factors, mass, level, jnp.zeros((LANES - groups - 2, LANES), f32)], axis=0
            )
            columns[a * rows : (a + 1) * rows, :] = jnp.transpose(tile)[:rows]

    turned = columns[pl.ds(pl.multiple_of(step * rows, rows), rows), :]
    wide = [jnp.broadcast_to(turned[:, g : g + 1], (rows, LANES)) for g in range(groups + 2)]
    mass, level = wide[groups], wide[groups + 1]
    weighted = jnp.zeros((rows, LANES), f32)
    for b in range(blocks):
        target = jnp.zeros((rows, LANES), f32)
        for g in range(groups):
            target = target + main_ref[g, pl.ds(b * rows, rows), :].astype(f32) * wide[g]
        logits = logits_ref[:, b * LANES : (b + 1) * LANES]
        weighted = weighted + target * logits
        share = jnp.exp(logits - level) * mass
        grad_ref = low_ref if b < blocks // 2 else high_ref
        at = b % (blocks // 2) * LANES
        grad_ref[:, at : at + LANES] = (loss_scale * (share - target)).astype(bf16)
    weighted = jnp.concatenate([weighted, jnp.zeros((LANES - rows, LANES), f32)], axis=0)
    lines[pl.ds(step, 1), :] = jnp.sum(jnp.transpose(weighted), axis=0, keepdims=True)

    @pl.when(step == chunks - 1)
    def _():
        @pl.loop(0, loss_ref.shape[0])
        def _(d):
            loss_ref[d] = lines[...]


def gradient_call(arrived, logits, group, rows, blocks):
    owners = arrived.shape[0]
    per = owners // group
    half, width = group * rows, blocks // 2 * LANES
    at = blocks * rows // STATS
    return pl.pallas_call(
        lambda *refs: gradient_kernel(*refs, blocks=blocks),
        grid=(group,),
        in_specs=[
            pl.BlockSpec((per, blocks * rows, LANES), lambda a: (a, 0, 0)),
            pl.BlockSpec((owners, STATS, LANES), lambda a: (0, at, 0)),
            pl.BlockSpec((rows, 2 * width), lambda a: (a, 0)),
        ],
        out_specs=[
            pl.BlockSpec((rows, width), lambda a: (a, 0)),
            pl.BlockSpec((rows, width), lambda a: (a, 0)),
            pl.BlockSpec((group, LANES), lambda a: (0, 0)),
            pl.BlockSpec((owners, group, LANES), lambda a: (0, 0, 0)),
        ],
        out_shape=[
            jax.ShapeDtypeStruct((half, width), bf16),
            jax.ShapeDtypeStruct((half, width), bf16),
            jax.ShapeDtypeStruct((group, LANES), f32),
            jax.ShapeDtypeStruct((owners, group, LANES), f32),
        ],
        scratch_shapes=[pltpu.VMEM((half, LANES), f32), pltpu.VMEM((group, LANES), f32)],
        cost_estimate=pl.CostEstimate(
            flops=20 * owners * blocks * rows * LANES,
            bytes_accessed=3 * owners * blocks * rows * LANES,
            transcendentals=2 * half * width,
        ),
        name="logit_gradient",
    )(arrived, arrived, logits)


def head_kernel(own_hidden, other_hidden, own_ref, other_ref, *refs):
    out_ref = refs[-1]
    total = jnp.dot(own_hidden[...], own_ref[...], preferred_element_type=f32)
    total += jnp.dot(other_hidden[...], other_ref[...], preferred_element_type=f32)
    out_ref[...] = total.astype(bf16)


def head_call(own_hidden, other_hidden, own, other, before):
    depth, half = own_hidden.shape
    width = own.shape[1]
    tile = 512
    column = 0 if before is None else 1
    hidden = pl.BlockSpec((tile, half), lambda i: (i, 0))
    grad = pl.BlockSpec((half, width), lambda i: (0, 0))
    extra = [] if before is None else [before]
    return pl.pallas_call(
        head_kernel,
        grid=(depth // tile,),
        in_specs=[hidden, hidden, grad, grad] + [pl.BlockSpec(memory_space=pl.ANY)] * len(extra),
        out_specs=pl.BlockSpec((tile, width), lambda i: (i, column)),
        out_shape=jax.ShapeDtypeStruct((depth, 2 * width), bf16),
        input_output_aliases={4: 0} if extra else {},
        cost_estimate=pl.CostEstimate(
            flops=4 * depth * half * width, bytes_accessed=6 * depth * half, transcendentals=0
        ),
        name="head_upper" if extra else "head_lower",
    )(own_hidden, other_hidden, own, other, *extra)


def coded(partial):
    step = jnp.max(jnp.abs(partial), axis=1, keepdims=True) / LEVELS
    inverse = jnp.where(step > 0, 1.0 / step, 0.0)
    return jnp.round(partial * inverse).astype(jnp.int32).astype(jnp.int16), step


def local(
    teacher_hidden,
    teacher_head,
    align_pos,
    pair_teacher,
    pair_student,
    align_values,
    student_hidden,
    student_head,
):
    pos = lax.axis_index("pos")
    group = lax.axis_size("tv")
    owners = group * lax.axis_size("sv")
    swap = [(0, 1), (1, 0)]
    count = align_pos.shape[0]
    half = count // 2
    pairs = pair_teacher.shape[0]
    width = teacher_head.shape[1]
    block = align_values.shape[1]
    blocks = student_head.shape[1] // block
    rows = half // group

    near = [align_values]
    for shift in (2, 6, 4):
        near.append(lax.ppermute(align_values, "tv", [(i, (i + shift) % group) for i in range(group)]))
    far = [lax.ppermute(v, "tv", [(i, i ^ 1) for i in range(group)]) for v in near]

    own, other = pos * half, (1 - pos) * half
    sent, sent_step = picked_logits(align_pos, teacher_hidden, teacher_head, other, half, True)
    own_at, other_at, sent_step = lax.optimization_barrier((own, other, sent_step))
    got = lax.ppermute(sent, "pos", swap)
    got_step = lax.ppermute(sent_step, "pos", swap)

    depth = student_hidden.shape[1]
    turned_own = jnp.transpose(lax.dynamic_slice(student_hidden, (own_at, 0), (half, depth)))
    turned_other = jnp.transpose(lax.dynamic_slice(student_hidden, (other_at, 0), (half, depth)))
    own_pos, turned_own = lax.optimization_barrier((align_pos, turned_own))
    (own_logits,) = picked_logits(own_pos, teacher_hidden, teacher_head, own, half, False)

    listed = jnp.stack([pair_teacher, pair_student // blocks, pair_student % blocks])
    listed = listed.astype(bf16)
    codes = jnp.pad(listed, ((0, rows - 3), (64, LANES - 64 - pairs)))
    row_sums = jnp.sum(align_values.astype(f32), axis=2)
    named = pair_teacher[None, :] == jnp.arange(width // block, dtype=jnp.int32)[:, None]
    reach = jnp.sum(jnp.where(named[:, :, None], row_sums[None], 0.0), axis=1).reshape(1, width)
    powers = pl.pallas_call(
        exp_kernel,
        grid=(group // 2,),
        in_specs=[
            pl.BlockSpec((2 * rows, width), lambda a: (a, 0)),
            pl.BlockSpec((2 * rows, width), lambda a: (a, 0)),
            pl.BlockSpec((group // 2, LANES), lambda a: (0, 0)),
            pl.BlockSpec((1, width), lambda a: (0, 0)),
            pl.BlockSpec((rows, LANES), lambda a: (0, 0)),
        ],
        out_specs=pl.BlockSpec((2 * rows, width + LANES), lambda a: (a, 0)),
        out_shape=jax.ShapeDtypeStruct((half, width + LANES), bf16),
        name="teacher_exp",
    )(own_logits, got, got_step, reach, codes)
    powers = lax.all_to_all(
        powers.reshape(group, rows, width + LANES), "tv", split_axis=0, concat_axis=0, tiled=True
    )

    def half_of(start):
        return lax.dynamic_slice(student_hidden, (start, 0), (half, student_hidden.shape[1]))

    student_sent, student_step = coded(
        jnp.dot(half_of(other), student_head, preferred_element_type=f32)
    )
    student_sent, student_step, _ = lax.optimization_barrier((student_sent, student_step, got))
    student_logits = jnp.dot(
        half_of(own), student_head, preferred_element_type=f32
    ) + lax.ppermute(student_sent, "pos", swap).astype(f32) * lax.ppermute(student_step, "pos", swap)
    peak = jnp.max(student_logits, axis=1)
    total = jnp.sum(jnp.exp(student_logits - peak[:, None]), axis=1)
    level = peak + jnp.log(total)
    student_tail = jnp.concatenate(
        [p.reshape(4, LANES) for p in pieces_outside(level)] + [jnp.zeros((4, LANES), f32)]
    ).astype(bf16)

    student_tail, turned_other = lax.optimization_barrier((student_tail, turned_other))

    place = lax.axis_index("tv")
    order = [place] + [(place - s) % group for s in (2, 6, 4)]
    order = jnp.stack(order + [o ^ 1 for o in order])
    listed = powers[:, 0:FIELDS, width + 64 : width + 64 + pairs].astype(jnp.int32).reshape(-1)
    values = near + far

    def exchange(x):
        return lax.all_to_all(x, ("tv", "sv"), split_axis=0, concat_axis=0, tiled=True)

    outgoing = product_call(listed, order, powers, student_tail, values, owners, blocks, width)
    arrived = exchange(outgoing)
    lower_grad, upper_grad, base, loss = gradient_call(arrived, student_logits, group, rows, blocks)
    lower_other = lax.ppermute(lower_grad, "pos", swap)
    upper_other = lax.ppermute(upper_grad, "pos", swap)
    weighted = exchange(loss)
    head_grad = head_call(turned_own, turned_other, lower_grad, lower_other, None)
    row_loss = (base - jnp.sum(weighted, axis=0))[:, :rows].reshape(half)
    head_grad = head_call(turned_own, turned_other, upper_grad, upper_other, head_grad)
    return (row_loss, head_grad)


def solution(mesh):
    placed = (
        P(None, "pos"),
        P("pos", ("tv", "sv")),
        P(),
        P(("tv", "sv")),
        P(("tv", "sv")),
        P(("tv", "sv"), None, None),
        P(None, "pos"),
        P("pos", ("tv", "sv")),
    )
    return jax.shard_map(
        local,
        mesh=mesh,
        in_specs=placed,
        out_specs=(P("pos"), P("pos", ("tv", "sv"))),
        check_vma=False,
    )
```

```python
import jax
import jax.numpy as jnp
from jax import lax
from jax.experimental import pallas as pl
from jax.experimental.pallas import tpu as pltpu
from jax.sharding import PartitionSpec as P


loss_scale = 1024.0
LANES = 128
LEVELS = 32767.0
f32, bf16 = jnp.float32, jnp.bfloat16


def pieces(x):
    hi = x.astype(bf16).astype(f32)
    mid = (x - hi).astype(bf16).astype(f32)
    low = (x - hi - mid).astype(bf16).astype(f32)
    return hi, mid, low


def pieces_outside(x):
    hi = lax.reduce_precision(x, 8, 7)
    mid = lax.reduce_precision(x - hi, 8, 7)
    low = lax.reduce_precision(x - hi - mid, 8, 7)
    return hi, mid, low


def lane_of(shape):
    return lax.broadcasted_iota(jnp.int32, shape, len(shape) - 1)


def column_tile(columns, rows):
    lane = lane_of((rows, LANES))
    tile = jnp.zeros((rows, LANES), f32)
    for i, column in enumerate(columns):
        tile = jnp.where(lane == i, column, tile)
    return tile


def picked_logits_kernel(
    first, at_scalar, at_ref, hidden_ref, head_ref, *refs, tile, coded_out
):
    outs, (near, chosen, picked, total) = refs[:-4], refs[-4:]
    step = pl.program_id(0)
    count, depth = hidden_ref.shape
    rows, window = near.shape
    tiles = rows // tile
    part = 256

    lows = [at_scalar[(first[0] + i) * tile] for i in range(tiles)]
    highs = [at_scalar[(first[0] + i) * tile + tile - 1] for i in range(tiles)]
    bases = [jnp.minimum(lax.div(low, 16) * 16, count - window) for low in lows]
    narrow = highs[0] < bases[0] + window
    for base, high in zip(bases[1:], highs[1:]):
        narrow = jnp.logical_and(narrow, high < base + window)

    @pl.when(step == 0)
    def _():
        for i in range(tiles):
            line = at_ref[pl.ds(first[0] + i, 1), :].astype(f32)
            at = jnp.transpose(jnp.broadcast_to(line, (tile, LANES))).astype(jnp.int32)
            lane = lane_of((tile, LANES))
            here = slice(i * tile, (i + 1) * tile)
            for j in range(window // LANES):
                near[here, j * LANES : (j + 1) * LANES] = (
                    (at == lane + (j * LANES + bases[i])).astype(f32).astype(bf16)
                )

            @pl.when(jnp.logical_not(narrow))
            def _():
                for j in range(count // LANES):
                    chosen[here, j * LANES : (j + 1) * LANES] = (
                        (at == lane + j * LANES).astype(f32).astype(bf16)
                    )

        total[...] = jnp.zeros_like(total)

    @pl.when(narrow)
    def _():
        for i in range(tiles):
            here = slice(i * tile, (i + 1) * tile)
            source = pl.ds(pl.multiple_of(bases[i], 16), window)
            picked[here, :] = jnp.dot(
                near[here, :], hidden_ref[source, :], preferred_element_type=f32
            ).astype(bf16)
        total[...] += jnp.dot(picked[...], head_ref[...], preferred_element_type=f32)

    @pl.when(jnp.logical_not(narrow))
    def _():
        @pl.loop(0, tiles)
        def _(i):
            here = pl.ds(pl.multiple_of(i * tile, tile), tile)
            low = lax.div(at_scalar[(first[0] + i) * tile], part)
            high = lax.div(at_scalar[(first[0] + i) * tile + tile - 1], part)
            picked[here, :] = jnp.zeros((tile, depth), bf16)

            @pl.loop(low, high + 1)
            def _(j):
                source = pl.ds(pl.multiple_of(j * part, part), part)
                found = jnp.dot(
                    chosen[here, source], hidden_ref[source, :], preferred_element_type=f32
                )
                picked[here, :] = (picked[here, :].astype(f32) + found).astype(bf16)

        @pl.loop(0, head_ref.shape[1] // 256)
        def _(j):
            here = pl.ds(pl.multiple_of(j * 256, 256), 256)
            total[:, here] += jnp.dot(picked[...], head_ref[:, here], preferred_element_type=f32)

    @pl.when(step == pl.num_programs(0) - 1)
    def _():
        if not coded_out:
            outs[0][...] = total[...]
            return
        for i in range(tiles):
            here = slice(i * tile, (i + 1) * tile)
            partial = total[here, :]
            step_size = jnp.max(jnp.abs(partial), axis=1, keepdims=True) / LEVELS
            inverse = jnp.where(step_size > 0, 1.0 / step_size, 0.0)
            outs[0][here, :] = jnp.round(partial * inverse).astype(jnp.int32).astype(jnp.int16)
            turned = jnp.transpose(jnp.broadcast_to(step_size, (tile, LANES)))
            outs[1][i : i + 1, :] = turned[0:1]


def picked_logits(align_pos, hidden, head, start, half, coded_out):
    count, depth = hidden.shape
    width = head.shape[1]
    tile, chunk = LANES, 1024
    shapes = [jax.ShapeDtypeStruct((half, width), jnp.int16 if coded_out else f32)]
    specs = [pl.BlockSpec((half, width), lambda k, *_: (0, 0))]
    if coded_out:
        shapes.append(jax.ShapeDtypeStruct((half // tile, LANES), f32))
        specs.append(pl.BlockSpec((half // tile, LANES), lambda k, *_: (0, 0)))
    return pl.pallas_call(
        lambda *refs: picked_logits_kernel(*refs, tile=tile, coded_out=coded_out),
        grid_spec=pltpu.PrefetchScalarGridSpec(
            num_scalar_prefetch=2,
            grid=(depth // chunk,),
            in_specs=[
                pl.BlockSpec((count // LANES, LANES), lambda k, *_: (0, 0)),
                pl.BlockSpec((count, chunk), lambda k, *_: (0, k)),
                pl.BlockSpec((chunk, width), lambda k, *_: (k, 0)),
            ],
            out_specs=specs,
            scratch_shapes=[
                pltpu.VMEM((half, min(256, count)), bf16),
                pltpu.VMEM((half, count), bf16),
                pltpu.VMEM((half, chunk), bf16),
                pltpu.VMEM((half, width), f32),
            ],
        ),
        out_shape=shapes,
        cost_estimate=pl.CostEstimate(
            flops=2 * half * depth * width + half * count * depth,
            bytes_accessed=2 * depth * (count + width) + 4 * half * width,
            transcendentals=0,
        ),
        name="teacher_sent" if coded_out else "teacher_own",
    )((start // tile).reshape(1), align_pos, align_pos.reshape(-1, LANES), hidden, head)


def exp_kernel(own_ref, sent_ref, step_ref, reach_ref, codes_ref, out_ref):
    rows, width = own_ref.shape
    line = step_ref[pl.ds(pl.program_id(0), 1), :]
    step_size = jnp.transpose(jnp.broadcast_to(line, (rows, LANES)))[:, 0:1]
    logits = own_ref[...] + sent_ref[...].astype(f32) * step_size
    peak = jnp.max(logits, axis=1, keepdims=True)
    powers = jnp.exp(logits - peak)
    total = jnp.sum(powers, axis=1, keepdims=True)
    out_ref[:, :width] = powers.astype(bf16)
    mass = jnp.sum(powers * reach_ref[...], axis=1, keepdims=True)
    stats = column_tile(pieces(peak) + pieces(total) + pieces(mass), rows)
    codes = jnp.concatenate([codes_ref[...].astype(f32)] * (rows // codes_ref.shape[0]), axis=0)
    out_ref[:, width:] = (stats + codes).astype(bf16)


FIELDS = 3
STATS = 16


def product_kernel(codes, source_of, powers_ref, student_ref, *refs, owners, pairs, blocks, width):
    values, out_ref = refs[:owners], refs[owners]
    held, total, weight, staged, sems, out_sems = refs[owners + 1 :]
    rows = powers_ref.shape[1]
    dests = out_ref.shape[0]
    for j in range(owners):
        pltpu.make_async_copy(values[j], held.at[j], sems.at[j]).start()

    chunk = blocks * rows

    @pl.loop(0, dests)
    def _(d):
        total[pl.ds(pl.multiple_of(d * chunk, chunk), chunk), :] = jnp.zeros((chunk, LANES), f32)

    couples = owners // 2
    peaks, sums, masses = [], [], []
    for q in range(couples):
        tiles = [
            powers_ref[source_of[2 * q + i], :, pl.ds(width, LANES)].astype(f32) for i in range(2)
        ]
        turned = jnp.transpose(jnp.concatenate(tiles, axis=0))
        peaks.append(turned[0:1] + turned[1:2] + turned[2:3])
        sums.append(turned[3:4] + turned[4:5] + turned[5:6])
        masses.append(turned[6:7] + turned[7:8] + turned[8:9])
    peak = peaks[0]
    for other in peaks[1:]:
        peak = jnp.maximum(peak, other)
    peak = jnp.maximum(peak, pltpu.roll(peak, rows, 1))
    factors = [jnp.exp(value - peak) for value in peaks]
    norm = sum(f * v for f, v in zip(factors, sums))
    norm = norm + pltpu.roll(norm, rows, 1)
    factors = [factor / norm for factor in factors]
    mass = sum(f * v for f, v in zip(factors, masses))
    mass = mass + pltpu.roll(mass, rows, 1)
    level = peak + jnp.log(norm)
    line = lax.broadcasted_iota(jnp.int32, (LANES, LANES), 0)
    square = jnp.zeros((LANES, LANES), f32)
    for q in range(couples):
        square = jnp.where(line == q, factors[q], square)
    turned = jnp.transpose(square)
    for j in range(owners):
        top = (j % 2) * rows
        weight[j] = jnp.broadcast_to(turned[top : top + rows, j // 2 : j // 2 + 1], (rows, LANES))

    found = pieces(level) + pieces(mass)
    left_half = lane_of((1, LANES)) < rows
    half_line = lax.broadcasted_iota(jnp.int32, (STATS, LANES), 0)
    stats = student_ref[...].astype(f32)
    for i in range(3):
        both = jnp.where(left_half, found[2 * i], found[2 * i + 1])
        stats = jnp.where(half_line == 12 + i, both, stats)
    stats = stats.astype(bf16)

    group = 8

    @pl.loop(0, owners)
    def _(j):
        pltpu.make_async_copy(values[0], held.at[j], sems.at[j]).wait()
        source = source_of[j]
        base = source * (FIELDS * pairs)

        @pl.loop(0, pairs // group)
        def _(i):
            products, places = [], []
            for u in range(group):
                at = i * group + u
                k = base + at
                left = powers_ref[source, :, pl.ds(pl.multiple_of(codes[k] * LANES, LANES), LANES)]
                products.append(jnp.dot(left, held[j, at], preferred_element_type=f32))
                spot = codes[k + pairs] * blocks + codes[k + 2 * pairs]
                places.append(pl.multiple_of(spot * rows, rows))
            scale = weight[j]
            for product, place in zip(products, places):
                total[pl.ds(place, rows), :] += product * scale

    batch = staged.shape[1]
    slots = staged.shape[0]

    def send(n):
        return pltpu.make_async_copy(
            staged.at[n % slots], out_ref.at[pl.ds(n * batch, batch)], out_sems.at[n % slots]
        )

    for n in range(dests // batch):
        if n >= slots:
            send(n - slots).wait()
        slot = n % slots

        @pl.loop(0, batch)
        def _(d):
            for b in range(blocks):
                at = ((n * batch + d) * blocks + b) * rows
                here = total[pl.ds(pl.multiple_of(at, rows), rows), :]
                staged[slot, d, pl.ds(b * rows, rows), :] = here.astype(bf16)
            staged[slot, d, pl.ds(chunk, STATS), :] = stats

        send(n).start()
    for n in range(dests // batch - slots, dests // batch):
        send(n).wait()


def product_call(codes, order, powers, tail, values, owners, blocks, width):
    group, rows, wide = powers.shape
    pairs, block = values[0].shape[:2]
    tall = blocks * rows + STATS
    return pl.pallas_call(
        lambda *refs: product_kernel(*refs, owners=group, pairs=pairs, blocks=blocks, width=width),
        grid_spec=pltpu.PrefetchScalarGridSpec(
            num_scalar_prefetch=2,
            grid=(1,),
            in_specs=[
                pl.BlockSpec((group, rows, wide), lambda i, *_: (0, 0, 0)),
                pl.BlockSpec((STATS, LANES), lambda i, *_: (0, 0)),
            ]
            + [pl.BlockSpec(memory_space=pl.ANY)] * group,
            out_specs=pl.BlockSpec(memory_space=pl.ANY),
            scratch_shapes=[
                pltpu.VMEM((group, pairs, block, block), bf16),
                pltpu.VMEM((owners * blocks * rows, LANES), f32),
                pltpu.VMEM((group, rows, LANES), f32),
                pltpu.VMEM((2, 8, tall, LANES), bf16),
                pltpu.SemaphoreType.DMA((group,)),
                pltpu.SemaphoreType.DMA((2,)),
            ],
        ),
        out_shape=jax.ShapeDtypeStruct((owners, tall, LANES), bf16),
        compiler_params=pltpu.CompilerParams(vmem_limit_bytes=48 << 20),
        cost_estimate=pl.CostEstimate(
            flops=40 * group * pairs * rows * block * block,
            bytes_accessed=2 * group * pairs * block * block + 2 * owners * tall * LANES,
            transcendentals=0,
        ),
        name="products",
    )(codes, order, powers, tail, *values)


def gradient_kernel(
    main_ref, all_ref, logits_ref, low_ref, high_ref, base_ref, loss_ref, columns, lines, *, blocks
):
    step = pl.program_id(0)
    rows = low_ref.shape[0]
    groups = main_ref.shape[0]
    chunks = all_ref.shape[0] // groups

    @pl.when(step == 0)
    def _():
        part = all_ref[...].astype(f32)
        levels = part[:, 0:4] + part[:, 4:8] + part[:, 8:12]
        peak = jnp.max(levels, axis=0)
        student = peak + jnp.log(jnp.sum(jnp.exp(levels - peak[None]), axis=0))
        other = pltpu.roll(student, rows, 1)
        first, second, third = part[:, 12, :], part[:, 13, :], part[:, 14, :]
        levels = first + pltpu.roll(first, rows, 1) + second
        masses = pltpu.roll(second, rows, 1) + third + pltpu.roll(third, rows, 1)
        for a in range(chunks):
            of = slice(a * groups, (a + 1) * groups)
            powers = jnp.exp(levels[of] - jnp.max(levels[of], axis=0, keepdims=True))
            factors = powers / jnp.sum(powers, axis=0, keepdims=True)
            mass = jnp.sum(masses[of] * factors, axis=0, keepdims=True)
            level = (other if a % 2 else student)[a // 2 : a // 2 + 1]
            base_ref[a : a + 1, :] = mass * level
            tile = jnp.concatenate(
                [factors, mass, level, jnp.zeros((LANES - groups - 2, LANES), f32)], axis=0
            )
            columns[a * rows : (a + 1) * rows, :] = jnp.transpose(tile)[:rows]

    strip = 16
    parts = []
    for r in range(0, rows, strip):
        turned = columns[pl.ds(pl.multiple_of(step * rows + r, strip), strip), :]
        wide = [jnp.broadcast_to(turned[:, g : g + 1], (strip, LANES)) for g in range(groups + 2)]
        mass, level = wide[groups], wide[groups + 1]
        weighted = jnp.zeros((strip, LANES), f32)
        for b in range(blocks):
            target = main_ref[0, pl.ds(b * rows + r, strip), :].astype(f32) * wide[0]
            for g in range(1, groups):
                target = target + main_ref[g, pl.ds(b * rows + r, strip), :].astype(f32) * wide[g]
            logits = logits_ref[r : r + strip, b * LANES : (b + 1) * LANES]
            weighted = weighted + target * logits
            share = jnp.exp(logits - level) * mass
            grad_ref = low_ref if b < blocks // 2 else high_ref
            at = b % (blocks // 2) * LANES
            grad_ref[r : r + strip, at : at + LANES] = (loss_scale * (share - target)).astype(bf16)
        parts.append(weighted)
    weighted = jnp.concatenate(parts, axis=0)
    weighted = jnp.concatenate([weighted, jnp.zeros((LANES - rows, LANES), f32)], axis=0)
    lines[pl.ds(step, 1), :] = jnp.sum(jnp.transpose(weighted), axis=0, keepdims=True)

    @pl.when(step == chunks - 1)
    def _():
        @pl.loop(0, loss_ref.shape[0])
        def _(d):
            loss_ref[d] = lines[...]


def gradient_call(arrived, logits, group, rows, blocks):
    owners = arrived.shape[0]
    per = owners // group
    half, width = group * rows, blocks // 2 * LANES
    at = blocks * rows // STATS
    return pl.pallas_call(
        lambda *refs: gradient_kernel(*refs, blocks=blocks),
        grid=(group,),
        in_specs=[
            pl.BlockSpec((per, blocks * rows, LANES), lambda a: (a, 0, 0)),
            pl.BlockSpec((owners, STATS, LANES), lambda a: (0, at, 0)),
            pl.BlockSpec((rows, 2 * width), lambda a: (a, 0)),
        ],
        out_specs=[
            pl.BlockSpec((rows, width), lambda a: (a, 0)),
            pl.BlockSpec((rows, width), lambda a: (a, 0)),
            pl.BlockSpec((group, LANES), lambda a: (0, 0)),
            pl.BlockSpec((owners, group, LANES), lambda a: (0, 0, 0)),
        ],
        out_shape=[
            jax.ShapeDtypeStruct((half, width), bf16),
            jax.ShapeDtypeStruct((half, width), bf16),
            jax.ShapeDtypeStruct((group, LANES), f32),
            jax.ShapeDtypeStruct((owners, group, LANES), f32),
        ],
        scratch_shapes=[pltpu.VMEM((half, LANES), f32), pltpu.VMEM((group, LANES), f32)],
        cost_estimate=pl.CostEstimate(
            flops=20 * owners * blocks * rows * LANES,
            bytes_accessed=3 * owners * blocks * rows * LANES,
            transcendentals=2 * half * width,
        ),
        name="logit_gradient",
    )(arrived, arrived, logits)


def head_kernel(own_hidden, other_hidden, own_ref, other_ref, *refs):
    out_ref = refs[-1]
    total = jnp.dot(own_hidden[...], own_ref[...], preferred_element_type=f32)
    total += jnp.dot(other_hidden[...], other_ref[...], preferred_element_type=f32)
    out_ref[...] = total.astype(bf16)


def head_call(own_hidden, other_hidden, own, other, before):
    depth, half = own_hidden.shape
    width = own.shape[1]
    tile = 512
    column = 0 if before is None else 1
    hidden = pl.BlockSpec((tile, half), lambda i: (i, 0))
    grad = pl.BlockSpec((half, width), lambda i: (0, 0))
    extra = [] if before is None else [before]
    return pl.pallas_call(
        head_kernel,
        grid=(depth // tile,),
        in_specs=[hidden, hidden, grad, grad] + [pl.BlockSpec(memory_space=pl.ANY)] * len(extra),
        out_specs=pl.BlockSpec((tile, width), lambda i: (i, column)),
        out_shape=jax.ShapeDtypeStruct((depth, 2 * width), bf16),
        input_output_aliases={4: 0} if extra else {},
        cost_estimate=pl.CostEstimate(
            flops=4 * depth * half * width, bytes_accessed=6 * depth * half, transcendentals=0
        ),
        name="head_upper" if extra else "head_lower",
    )(own_hidden, other_hidden, own, other, *extra)


def coded(partial):
    step = jnp.max(jnp.abs(partial), axis=1, keepdims=True) / LEVELS
    inverse = jnp.where(step > 0, 1.0 / step, 0.0)
    return jnp.round(partial * inverse).astype(jnp.int32).astype(jnp.int16), step


def local(
    teacher_hidden,
    teacher_head,
    align_pos,
    pair_teacher,
    pair_student,
    align_values,
    student_hidden,
    student_head,
):
    pos = lax.axis_index("pos")
    group = lax.axis_size("tv")
    owners = group * lax.axis_size("sv")
    swap = [(0, 1), (1, 0)]
    count = align_pos.shape[0]
    half = count // 2
    pairs = pair_teacher.shape[0]
    width = teacher_head.shape[1]
    block = align_values.shape[1]
    blocks = student_head.shape[1] // block
    rows = half // group

    near = [align_values]
    for shift in (2, 6, 4):
        near.append(lax.ppermute(align_values, "tv", [(i, (i + shift) % group) for i in range(group)]))
    far = [lax.ppermute(v, "tv", [(i, i ^ 1) for i in range(group)]) for v in near]

    own, other = pos * half, (1 - pos) * half
    sent, sent_step = picked_logits(align_pos, teacher_hidden, teacher_head, other, half, True)
    own_at, other_at, sent_step = lax.optimization_barrier((own, other, sent_step))
    got = lax.ppermute(sent, "pos", swap)
    got_step = lax.ppermute(sent_step, "pos", swap)

    depth = student_hidden.shape[1]
    turned_own = jnp.transpose(lax.dynamic_slice(student_hidden, (own_at, 0), (half, depth)))
    turned_other = jnp.transpose(lax.dynamic_slice(student_hidden, (other_at, 0), (half, depth)))
    own_pos, turned_own = lax.optimization_barrier((align_pos, turned_own))
    (own_logits,) = picked_logits(own_pos, teacher_hidden, teacher_head, own, half, False)

    listed = jnp.stack([pair_teacher, pair_student // blocks, pair_student % blocks])
    listed = listed.astype(bf16)
    codes = jnp.pad(listed, ((0, rows - 3), (64, LANES - 64 - pairs)))
    row_sums = jnp.sum(align_values.astype(f32), axis=2)
    named = pair_teacher[None, :] == jnp.arange(width // block, dtype=jnp.int32)[:, None]
    reach = jnp.sum(jnp.where(named[:, :, None], row_sums[None], 0.0), axis=1).reshape(1, width)
    powers = pl.pallas_call(
        exp_kernel,
        grid=(group // 2,),
        in_specs=[
            pl.BlockSpec((2 * rows, width), lambda a: (a, 0)),
            pl.BlockSpec((2 * rows, width), lambda a: (a, 0)),
            pl.BlockSpec((group // 2, LANES), lambda a: (0, 0)),
            pl.BlockSpec((1, width), lambda a: (0, 0)),
            pl.BlockSpec((rows, LANES), lambda a: (0, 0)),
        ],
        out_specs=pl.BlockSpec((2 * rows, width + LANES), lambda a: (a, 0)),
        out_shape=jax.ShapeDtypeStruct((half, width + LANES), bf16),
        name="teacher_exp",
    )(own_logits, got, got_step, reach, codes)
    powers = lax.all_to_all(
        powers.reshape(group, rows, width + LANES), "tv", split_axis=0, concat_axis=0, tiled=True
    )

    def half_of(start):
        return lax.dynamic_slice(student_hidden, (start, 0), (half, student_hidden.shape[1]))

    student_sent, student_step = coded(
        jnp.dot(half_of(other), student_head, preferred_element_type=f32)
    )
    student_sent, student_step, _ = lax.optimization_barrier((student_sent, student_step, got))
    student_logits = jnp.dot(
        half_of(own), student_head, preferred_element_type=f32
    ) + lax.ppermute(student_sent, "pos", swap).astype(f32) * lax.ppermute(student_step, "pos", swap)
    peak = jnp.max(student_logits, axis=1)
    total = jnp.sum(jnp.exp(student_logits - peak[:, None]), axis=1)
    level = peak + jnp.log(total)
    student_tail = jnp.concatenate(
        [p.reshape(4, LANES) for p in pieces_outside(level)] + [jnp.zeros((4, LANES), f32)]
    ).astype(bf16)

    student_tail, turned_other = lax.optimization_barrier((student_tail, turned_other))

    place = lax.axis_index("tv")
    order = [place] + [(place - s) % group for s in (2, 6, 4)]
    order = jnp.stack(order + [o ^ 1 for o in order])
    listed = powers[:, 0:FIELDS, width + 64 : width + 64 + pairs].astype(jnp.int32).reshape(-1)
    values = near + far

    def exchange(x):
        return lax.all_to_all(x, ("tv", "sv"), split_axis=0, concat_axis=0, tiled=True)

    outgoing = product_call(listed, order, powers, student_tail, values, owners, blocks, width)
    arrived = exchange(outgoing)
    lower_grad, upper_grad, base, loss = gradient_call(arrived, student_logits, group, rows, blocks)
    lower_other = lax.ppermute(lower_grad, "pos", swap)
    upper_other = lax.ppermute(upper_grad, "pos", swap)
    weighted = exchange(loss)
    head_grad = head_call(turned_own, turned_other, lower_grad, lower_other, None)
    weighted, head_grad = lax.optimization_barrier((weighted, head_grad))
    row_loss = (base - jnp.sum(weighted, axis=0))[:, :rows].reshape(half)
    head_grad = head_call(turned_own, turned_other, upper_grad, upper_other, head_grad)
    return (row_loss, head_grad)


def solution(mesh):
    placed = (
        P(None, "pos"),
        P("pos", ("tv", "sv")),
        P(),
        P(("tv", "sv")),
        P(("tv", "sv")),
        P(("tv", "sv"), None, None),
        P(None, "pos"),
        P("pos", ("tv", "sv")),
    )
    return jax.shard_map(
        local,
        mesh=mesh,
        in_specs=placed,
        out_specs=(P("pos"), P("pos", ("tv", "sv"))),
        check_vma=False,
    )
```

```python
import jax
import jax.numpy as jnp
from jax import lax
from jax.experimental import pallas as pl
from jax.experimental.pallas import tpu as pltpu
from jax.sharding import PartitionSpec as P


loss_scale = 1024.0
LANES = 128
LEVELS = 32767.0
f32, bf16 = jnp.float32, jnp.bfloat16


def pieces(x):
    hi = x.astype(bf16).astype(f32)
    mid = (x - hi).astype(bf16).astype(f32)
    low = (x - hi - mid).astype(bf16).astype(f32)
    return hi, mid, low


def pieces_outside(x):
    hi = lax.reduce_precision(x, 8, 7)
    mid = lax.reduce_precision(x - hi, 8, 7)
    low = lax.reduce_precision(x - hi - mid, 8, 7)
    return hi, mid, low


def lane_of(shape):
    return lax.broadcasted_iota(jnp.int32, shape, len(shape) - 1)


def column_tile(columns, rows):
    lane = lane_of((rows, LANES))
    tile = jnp.zeros((rows, LANES), f32)
    for i, column in enumerate(columns):
        tile = jnp.where(lane == i, column, tile)
    return tile


def picked_logits_kernel(
    first, at_scalar, at_ref, hidden_ref, head_ref, *refs, tile, coded_out
):
    outs, (near, chosen, picked, total) = refs[:-4], refs[-4:]
    step = pl.program_id(0)
    count, depth = hidden_ref.shape
    rows, window = near.shape
    tiles = rows // tile
    part = 256

    lows = [at_scalar[(first[0] + i) * tile] for i in range(tiles)]
    highs = [at_scalar[(first[0] + i) * tile + tile - 1] for i in range(tiles)]
    bases = [jnp.minimum(lax.div(low, 16) * 16, count - window) for low in lows]
    narrow = highs[0] < bases[0] + window
    for base, high in zip(bases[1:], highs[1:]):
        narrow = jnp.logical_and(narrow, high < base + window)

    @pl.when(step == 0)
    def _():
        for i in range(tiles):
            line = at_ref[pl.ds(first[0] + i, 1), :].astype(f32)
            at = jnp.transpose(jnp.broadcast_to(line, (tile, LANES))).astype(jnp.int32)
            lane = lane_of((tile, LANES))
            here = slice(i * tile, (i + 1) * tile)
            for j in range(window // LANES):
                near[here, j * LANES : (j + 1) * LANES] = (
                    (at == lane + (j * LANES + bases[i])).astype(f32).astype(bf16)
                )

            @pl.when(jnp.logical_not(narrow))
            def _():
                for j in range(count // LANES):
                    chosen[here, j * LANES : (j + 1) * LANES] = (
                        (at == lane + j * LANES).astype(f32).astype(bf16)
                    )

        total[...] = jnp.zeros_like(total)

    @pl.when(narrow)
    def _():
        for i in range(tiles):
            here = slice(i * tile, (i + 1) * tile)
            source = pl.ds(pl.multiple_of(bases[i], 16), window)
            picked[here, :] = jnp.dot(
                near[here, :], hidden_ref[source, :], preferred_element_type=f32
            ).astype(bf16)
        total[...] += jnp.dot(picked[...], head_ref[...], preferred_element_type=f32)

    @pl.when(jnp.logical_not(narrow))
    def _():
        @pl.loop(0, tiles)
        def _(i):
            here = pl.ds(pl.multiple_of(i * tile, tile), tile)
            low = lax.div(at_scalar[(first[0] + i) * tile], part)
            high = lax.div(at_scalar[(first[0] + i) * tile + tile - 1], part)
            picked[here, :] = jnp.zeros((tile, depth), bf16)

            @pl.loop(low, high + 1)
            def _(j):
                source = pl.ds(pl.multiple_of(j * part, part), part)
                found = jnp.dot(
                    chosen[here, source], hidden_ref[source, :], preferred_element_type=f32
                )
                picked[here, :] = (picked[here, :].astype(f32) + found).astype(bf16)

        @pl.loop(0, head_ref.shape[1] // 256)
        def _(j):
            here = pl.ds(pl.multiple_of(j * 256, 256), 256)
            total[:, here] += jnp.dot(picked[...], head_ref[:, here], preferred_element_type=f32)

    @pl.when(step == pl.num_programs(0) - 1)
    def _():
        if not coded_out:
            outs[0][...] = total[...]
            return
        for i in range(tiles):
            here = slice(i * tile, (i + 1) * tile)
            partial = total[here, :]
            step_size = jnp.max(jnp.abs(partial), axis=1, keepdims=True) / LEVELS
            inverse = jnp.where(step_size > 0, 1.0 / step_size, 0.0)
            outs[0][here, :] = jnp.round(partial * inverse).astype(jnp.int32).astype(jnp.int16)
            turned = jnp.transpose(jnp.broadcast_to(step_size, (tile, LANES)))
            outs[1][i : i + 1, :] = turned[0:1]


def picked_logits(align_pos, hidden, head, start, half, coded_out):
    count, depth = hidden.shape
    width = head.shape[1]
    tile, chunk = LANES, 1024
    shapes = [jax.ShapeDtypeStruct((half, width), jnp.int16 if coded_out else f32)]
    specs = [pl.BlockSpec((half, width), lambda k, *_: (0, 0))]
    if coded_out:
        shapes.append(jax.ShapeDtypeStruct((half // tile, LANES), f32))
        specs.append(pl.BlockSpec((half // tile, LANES), lambda k, *_: (0, 0)))
    return pl.pallas_call(
        lambda *refs: picked_logits_kernel(*refs, tile=tile, coded_out=coded_out),
        grid_spec=pltpu.PrefetchScalarGridSpec(
            num_scalar_prefetch=2,
            grid=(depth // chunk,),
            in_specs=[
                pl.BlockSpec((count // LANES, LANES), lambda k, *_: (0, 0)),
                pl.BlockSpec((count, chunk), lambda k, *_: (0, k)),
                pl.BlockSpec((chunk, width), lambda k, *_: (k, 0)),
            ],
            out_specs=specs,
            scratch_shapes=[
                pltpu.VMEM((half, min(256, count)), bf16),
                pltpu.VMEM((half, count), bf16),
                pltpu.VMEM((half, chunk), bf16),
                pltpu.VMEM((half, width), f32),
            ],
        ),
        out_shape=shapes,
        cost_estimate=pl.CostEstimate(
            flops=2 * half * depth * width + half * count * depth,
            bytes_accessed=2 * depth * (count + width) + 4 * half * width,
            transcendentals=0,
        ),
        name="teacher_sent" if coded_out else "teacher_own",
    )((start // tile).reshape(1), align_pos, align_pos.reshape(-1, LANES), hidden, head)


def exp_kernel(own_ref, sent_ref, step_ref, reach_ref, codes_ref, out_ref):
    rows, width = own_ref.shape
    line = step_ref[pl.ds(pl.program_id(0), 1), :]
    step_size = jnp.transpose(jnp.broadcast_to(line, (rows, LANES)))[:, 0:1]
    logits = own_ref[...] + sent_ref[...].astype(f32) * step_size
    peak = jnp.max(logits, axis=1, keepdims=True)
    powers = jnp.exp(logits - peak)
    total = jnp.sum(powers, axis=1, keepdims=True)
    out_ref[:, :width] = powers.astype(bf16)
    mass = jnp.sum(powers * reach_ref[...], axis=1, keepdims=True)
    stats = column_tile(pieces(peak) + pieces(total) + pieces(mass), rows)
    codes = jnp.concatenate([codes_ref[...].astype(f32)] * (rows // codes_ref.shape[0]), axis=0)
    out_ref[:, width:] = (stats + codes).astype(bf16)


FIELDS = 3
STATS = 16


def product_kernel(codes, source_of, powers_ref, student_ref, *refs, owners, pairs, blocks, width):
    values, out_ref = refs[:owners], refs[owners]
    held, total, weight, staged, sems, out_sems = refs[owners + 1 :]
    rows = powers_ref.shape[1]
    dests = out_ref.shape[0]
    for j in range(owners):
        pltpu.make_async_copy(values[j], held.at[j], sems.at[j]).start()

    chunk = blocks * rows

    @pl.loop(0, dests)
    def _(d):
        total[pl.ds(pl.multiple_of(d * chunk, chunk), chunk), :] = jnp.zeros((chunk, LANES), f32)

    couples = owners // 2
    peaks, sums, masses = [], [], []
    for q in range(couples):
        tiles = [
            powers_ref[source_of[2 * q + i], :, pl.ds(width, LANES)].astype(f32) for i in range(2)
        ]
        turned = jnp.transpose(jnp.concatenate(tiles, axis=0))
        peaks.append(turned[0:1] + turned[1:2] + turned[2:3])
        sums.append(turned[3:4] + turned[4:5] + turned[5:6])
        masses.append(turned[6:7] + turned[7:8] + turned[8:9])
    peak = peaks[0]
    for other in peaks[1:]:
        peak = jnp.maximum(peak, other)
    peak = jnp.maximum(peak, pltpu.roll(peak, rows, 1))
    factors = [jnp.exp(value - peak) for value in peaks]
    norm = sum(f * v for f, v in zip(factors, sums))
    norm = norm + pltpu.roll(norm, rows, 1)
    factors = [factor / norm for factor in factors]
    mass = sum(f * v for f, v in zip(factors, masses))
    mass = mass + pltpu.roll(mass, rows, 1)
    level = peak + jnp.log(norm)
    line = lax.broadcasted_iota(jnp.int32, (LANES, LANES), 0)
    square = jnp.zeros((LANES, LANES), f32)
    for q in range(couples):
        square = jnp.where(line == q, factors[q], square)
    turned = jnp.transpose(square)
    for j in range(owners):
        top = (j % 2) * rows
        weight[j] = jnp.broadcast_to(turned[top : top + rows, j // 2 : j // 2 + 1], (rows, LANES))

    found = pieces(level) + pieces(mass)
    left_half = lane_of((1, LANES)) < rows
    half_line = lax.broadcasted_iota(jnp.int32, (STATS, LANES), 0)
    stats = student_ref[...].astype(f32)
    for i in range(3):
        both = jnp.where(left_half, found[2 * i], found[2 * i + 1])
        stats = jnp.where(half_line == 12 + i, both, stats)
    stats = stats.astype(bf16)

    group = 8

    @pl.loop(0, owners)
    def _(j):
        pltpu.make_async_copy(values[0], held.at[j], sems.at[j]).wait()
        source = source_of[j]
        base = source * (FIELDS * pairs)

        @pl.loop(0, pairs // group)
        def _(i):
            products, places = [], []
            for u in range(group):
                at = i * group + u
                k = base + at
                left = powers_ref[source, :, pl.ds(pl.multiple_of(codes[k] * LANES, LANES), LANES)]
                products.append(jnp.dot(left, held[j, at], preferred_element_type=f32))
                spot = codes[k + pairs] * blocks + codes[k + 2 * pairs]
                places.append(pl.multiple_of(spot * rows, rows))
            scale = weight[j]
            for product, place in zip(products, places):
                total[pl.ds(place, rows), :] += product * scale

    batch = staged.shape[1]
    slots = staged.shape[0]

    def send(n):
        return pltpu.make_async_copy(
            staged.at[n % slots], out_ref.at[pl.ds(n * batch, batch)], out_sems.at[n % slots]
        )

    for n in range(dests // batch):
        if n >= slots:
            send(n - slots).wait()
        slot = n % slots

        @pl.loop(0, batch)
        def _(d):
            for b in range(blocks):
                at = ((n * batch + d) * blocks + b) * rows
                here = total[pl.ds(pl.multiple_of(at, rows), rows), :]
                staged[slot, d, pl.ds(b * rows, rows), :] = here.astype(bf16)
            staged[slot, d, pl.ds(chunk, STATS), :] = stats

        send(n).start()
    for n in range(dests // batch - slots, dests // batch):
        send(n).wait()


def product_call(codes, order, powers, tail, values, owners, blocks, width):
    group, rows, wide = powers.shape
    pairs, block = values[0].shape[:2]
    tall = blocks * rows + STATS
    return pl.pallas_call(
        lambda *refs: product_kernel(*refs, owners=group, pairs=pairs, blocks=blocks, width=width),
        grid_spec=pltpu.PrefetchScalarGridSpec(
            num_scalar_prefetch=2,
            grid=(1,),
            in_specs=[
                pl.BlockSpec((group, rows, wide), lambda i, *_: (0, 0, 0)),
                pl.BlockSpec((STATS, LANES), lambda i, *_: (0, 0)),
            ]
            + [pl.BlockSpec(memory_space=pl.ANY)] * group,
            out_specs=pl.BlockSpec(memory_space=pl.ANY),
            scratch_shapes=[
                pltpu.VMEM((group, pairs, block, block), bf16),
                pltpu.VMEM((owners * blocks * rows, LANES), f32),
                pltpu.VMEM((group, rows, LANES), f32),
                pltpu.VMEM((2, 8, tall, LANES), bf16),
                pltpu.SemaphoreType.DMA((group,)),
                pltpu.SemaphoreType.DMA((2,)),
            ],
        ),
        out_shape=jax.ShapeDtypeStruct((owners, tall, LANES), bf16),
        compiler_params=pltpu.CompilerParams(vmem_limit_bytes=60 << 20),
        cost_estimate=pl.CostEstimate(
            flops=40 * group * pairs * rows * block * block,
            bytes_accessed=2 * group * pairs * block * block + 2 * owners * tall * LANES,
            transcendentals=0,
        ),
        name="products",
    )(codes, order, powers, tail, *values)


def gradient_kernel(
    main_ref, all_ref, logits_ref, low_ref, high_ref, base_ref, loss_ref, columns, lines, *, blocks
):
    step = pl.program_id(0)
    rows = low_ref.shape[0]
    groups = main_ref.shape[0]
    chunks = all_ref.shape[0] // groups

    @pl.when(step == 0)
    def _():
        part = all_ref[...].astype(f32)
        levels = part[:, 0:4] + part[:, 4:8] + part[:, 8:12]
        peak = jnp.max(levels, axis=0)
        student = peak + jnp.log(jnp.sum(jnp.exp(levels - peak[None]), axis=0))
        other = pltpu.roll(student, rows, 1)
        first, second, third = part[:, 12, :], part[:, 13, :], part[:, 14, :]
        levels = first + pltpu.roll(first, rows, 1) + second
        masses = pltpu.roll(second, rows, 1) + third + pltpu.roll(third, rows, 1)
        for a in range(chunks):
            of = slice(a * groups, (a + 1) * groups)
            powers = jnp.exp(levels[of] - jnp.max(levels[of], axis=0, keepdims=True))
            factors = powers / jnp.sum(powers, axis=0, keepdims=True)
            mass = jnp.sum(masses[of] * factors, axis=0, keepdims=True)
            level = (other if a % 2 else student)[a // 2 : a // 2 + 1]
            base_ref[a : a + 1, :] = mass * level
            tile = jnp.concatenate(
                [factors, mass, level, jnp.zeros((LANES - groups - 2, LANES), f32)], axis=0
            )
            columns[a * rows : (a + 1) * rows, :] = jnp.transpose(tile)[:rows]

    strip = 16
    parts = []
    for r in range(0, rows, strip):
        turned = columns[pl.ds(pl.multiple_of(step * rows + r, strip), strip), :]
        wide = [jnp.broadcast_to(turned[:, g : g + 1], (strip, LANES)) for g in range(groups + 2)]
        mass, level = wide[groups], wide[groups + 1]
        weighted = jnp.zeros((strip, LANES), f32)
        for b in range(blocks):
            target = main_ref[0, pl.ds(b * rows + r, strip), :].astype(f32) * wide[0]
            for g in range(1, groups):
                target = target + main_ref[g, pl.ds(b * rows + r, strip), :].astype(f32) * wide[g]
            logits = logits_ref[r : r + strip, b * LANES : (b + 1) * LANES]
            weighted = weighted + target * logits
            share = jnp.exp(logits - level) * mass
            grad_ref = low_ref if b < blocks // 2 else high_ref
            at = b % (blocks // 2) * LANES
            grad_ref[r : r + strip, at : at + LANES] = (loss_scale * (share - target)).astype(bf16)
        parts.append(weighted)
    weighted = jnp.concatenate(parts, axis=0)
    weighted = jnp.concatenate([weighted, jnp.zeros((LANES - rows, LANES), f32)], axis=0)
    lines[pl.ds(step, 1), :] = jnp.sum(jnp.transpose(weighted), axis=0, keepdims=True)

    @pl.when(step == chunks - 1)
    def _():
        @pl.loop(0, loss_ref.shape[0])
        def _(d):
            loss_ref[d] = lines[...]


def gradient_call(arrived, logits, group, rows, blocks):
    owners = arrived.shape[0]
    per = owners // group
    half, width = group * rows, blocks // 2 * LANES
    at = blocks * rows // STATS
    return pl.pallas_call(
        lambda *refs: gradient_kernel(*refs, blocks=blocks),
        grid=(group,),
        in_specs=[
            pl.BlockSpec((per, blocks * rows, LANES), lambda a: (a, 0, 0)),
            pl.BlockSpec((owners, STATS, LANES), lambda a: (0, at, 0)),
            pl.BlockSpec((rows, 2 * width), lambda a: (a, 0)),
        ],
        out_specs=[
            pl.BlockSpec((rows, width), lambda a: (a, 0)),
            pl.BlockSpec((rows, width), lambda a: (a, 0)),
            pl.BlockSpec((group, LANES), lambda a: (0, 0)),
            pl.BlockSpec((owners, group, LANES), lambda a: (0, 0, 0)),
        ],
        out_shape=[
            jax.ShapeDtypeStruct((half, width), bf16),
            jax.ShapeDtypeStruct((half, width), bf16),
            jax.ShapeDtypeStruct((group, LANES), f32),
            jax.ShapeDtypeStruct((owners, group, LANES), f32),
        ],
        scratch_shapes=[pltpu.VMEM((half, LANES), f32), pltpu.VMEM((group, LANES), f32)],
        cost_estimate=pl.CostEstimate(
            flops=20 * owners * blocks * rows * LANES,
            bytes_accessed=3 * owners * blocks * rows * LANES,
            transcendentals=2 * half * width,
        ),
        compiler_params=pltpu.CompilerParams(vmem_limit_bytes=16 << 20),
        name="logit_gradient",
    )(arrived, arrived, logits)


def head_kernel(own_hidden, other_hidden, own_ref, other_ref, *refs):
    out_ref = refs[-1]
    total = jnp.dot(own_hidden[...], own_ref[...], preferred_element_type=f32)
    total += jnp.dot(other_hidden[...], other_ref[...], preferred_element_type=f32)
    out_ref[...] = total.astype(bf16)


def head_call(own_hidden, other_hidden, own, other, before):
    depth, half = own_hidden.shape
    width = own.shape[1]
    tile = 512
    column = 0 if before is None else 1
    hidden = pl.BlockSpec((tile, half), lambda i: (i, 0))
    grad = pl.BlockSpec((half, width), lambda i: (0, 0))
    extra = [] if before is None else [before]
    return pl.pallas_call(
        head_kernel,
        grid=(depth // tile,),
        in_specs=[hidden, hidden, grad, grad] + [pl.BlockSpec(memory_space=pl.ANY)] * len(extra),
        out_specs=pl.BlockSpec((tile, width), lambda i: (i, column)),
        out_shape=jax.ShapeDtypeStruct((depth, 2 * width), bf16),
        input_output_aliases={4: 0} if extra else {},
        cost_estimate=pl.CostEstimate(
            flops=4 * depth * half * width, bytes_accessed=6 * depth * half, transcendentals=0
        ),
        name="head_upper" if extra else "head_lower",
    )(own_hidden, other_hidden, own, other, *extra)


def coded(partial):
    step = jnp.max(jnp.abs(partial), axis=1, keepdims=True) / LEVELS
    inverse = jnp.where(step > 0, 1.0 / step, 0.0)
    return jnp.round(partial * inverse).astype(jnp.int32).astype(jnp.int16), step


def local(
    teacher_hidden,
    teacher_head,
    align_pos,
    pair_teacher,
    pair_student,
    align_values,
    student_hidden,
    student_head,
):
    pos = lax.axis_index("pos")
    group = lax.axis_size("tv")
    owners = group * lax.axis_size("sv")
    swap = [(0, 1), (1, 0)]
    count = align_pos.shape[0]
    half = count // 2
    pairs = pair_teacher.shape[0]
    width = teacher_head.shape[1]
    block = align_values.shape[1]
    blocks = student_head.shape[1] // block
    rows = half // group

    near = [align_values]
    for shift in (2, 6, 4):
        near.append(lax.ppermute(align_values, "tv", [(i, (i + shift) % group) for i in range(group)]))
    far = [lax.ppermute(v, "tv", [(i, i ^ 1) for i in range(group)]) for v in near]

    own, other = pos * half, (1 - pos) * half
    sent, sent_step = picked_logits(align_pos, teacher_hidden, teacher_head, other, half, True)
    own_at, other_at, sent_step = lax.optimization_barrier((own, other, sent_step))
    got = lax.ppermute(sent, "pos", swap)
    got_step = lax.ppermute(sent_step, "pos", swap)

    depth = student_hidden.shape[1]
    turned_own = jnp.transpose(lax.dynamic_slice(student_hidden, (own_at, 0), (half, depth)))
    turned_other = jnp.transpose(lax.dynamic_slice(student_hidden, (other_at, 0), (half, depth)))
    own_pos, turned_own = lax.optimization_barrier((align_pos, turned_own))
    (own_logits,) = picked_logits(own_pos, teacher_hidden, teacher_head, own, half, False)

    listed = jnp.stack([pair_teacher, pair_student // blocks, pair_student % blocks])
    listed = listed.astype(bf16)
    codes = jnp.pad(listed, ((0, rows - 3), (64, LANES - 64 - pairs)))
    row_sums = jnp.sum(align_values.astype(f32), axis=2)
    named = pair_teacher[None, :] == jnp.arange(width // block, dtype=jnp.int32)[:, None]
    reach = jnp.sum(jnp.where(named[:, :, None], row_sums[None], 0.0), axis=1).reshape(1, width)
    powers = pl.pallas_call(
        exp_kernel,
        grid=(group // 2,),
        in_specs=[
            pl.BlockSpec((2 * rows, width), lambda a: (a, 0)),
            pl.BlockSpec((2 * rows, width), lambda a: (a, 0)),
            pl.BlockSpec((group // 2, LANES), lambda a: (0, 0)),
            pl.BlockSpec((1, width), lambda a: (0, 0)),
            pl.BlockSpec((rows, LANES), lambda a: (0, 0)),
        ],
        out_specs=pl.BlockSpec((2 * rows, width + LANES), lambda a: (a, 0)),
        out_shape=jax.ShapeDtypeStruct((half, width + LANES), bf16),
        name="teacher_exp",
    )(own_logits, got, got_step, reach, codes)
    powers = lax.all_to_all(
        powers.reshape(group, rows, width + LANES), "tv", split_axis=0, concat_axis=0, tiled=True
    )

    def half_of(start):
        return lax.dynamic_slice(student_hidden, (start, 0), (half, student_hidden.shape[1]))

    student_sent, student_step = coded(
        jnp.dot(half_of(other), student_head, preferred_element_type=f32)
    )
    student_sent, student_step, _ = lax.optimization_barrier((student_sent, student_step, got))
    student_logits = jnp.dot(
        half_of(own), student_head, preferred_element_type=f32
    ) + lax.ppermute(student_sent, "pos", swap).astype(f32) * lax.ppermute(student_step, "pos", swap)
    peak = jnp.max(student_logits, axis=1)
    total = jnp.sum(jnp.exp(student_logits - peak[:, None]), axis=1)
    level = peak + jnp.log(total)
    student_tail = jnp.concatenate(
        [p.reshape(4, LANES) for p in pieces_outside(level)] + [jnp.zeros((4, LANES), f32)]
    ).astype(bf16)

    student_tail, turned_other = lax.optimization_barrier((student_tail, turned_other))

    place = lax.axis_index("tv")
    order = [place] + [(place - s) % group for s in (2, 6, 4)]
    order = jnp.stack(order + [o ^ 1 for o in order])
    listed = powers[:, 0:FIELDS, width + 64 : width + 64 + pairs].astype(jnp.int32).reshape(-1)
    values = near + far

    def exchange(x):
        return lax.all_to_all(x, ("tv", "sv"), split_axis=0, concat_axis=0, tiled=True)

    outgoing = product_call(listed, order, powers, student_tail, values, owners, blocks, width)
    arrived = exchange(outgoing)
    lower_grad, upper_grad, base, loss = gradient_call(arrived, student_logits, group, rows, blocks)
    lower_other = lax.ppermute(lower_grad, "pos", swap)
    upper_other = lax.ppermute(upper_grad, "pos", swap)
    weighted = exchange(loss)
    head_grad = head_call(turned_own, turned_other, lower_grad, lower_other, None)
    head_grad = head_call(turned_own, turned_other, upper_grad, upper_other, head_grad)
    weighted, head_grad = lax.optimization_barrier((weighted, head_grad))
    row_loss = (base - jnp.sum(weighted, axis=0))[:, :rows].reshape(half)
    return (row_loss, head_grad)


def solution(mesh):
    placed = (
        P(None, "pos"),
        P("pos", ("tv", "sv")),
        P(),
        P(("tv", "sv")),
        P(("tv", "sv")),
        P(("tv", "sv"), None, None),
        P(None, "pos"),
        P("pos", ("tv", "sv")),
    )
    return jax.shard_map(
        local,
        mesh=mesh,
        in_specs=placed,
        out_specs=(P("pos"), P("pos", ("tv", "sv"))),
        check_vma=False,
    )
```
